32 devices in a mesh: dp: 16 (over z, y, core), tensor: 2 (over x).
Axes of the slice: x: 2, y: 2, z: 4, core: 2. Of those that a mesh axis runs over, the one named last changes fastest.
Arguments:
- inputs: bfloat16 [2, 16384, 768], P(None, ('dp', 'tensor')), may hold values from -6 to 6
- cotangent: bfloat16 [2, 16384, 768], P(None, ('dp', 'tensor')), may hold values from -6 to 6
- seg_ids: int32 [2, 16, 512], P(None, 'dp'), may hold values from 0 to 3, never falling along the last dimension, each value on 1 to 192 neighbouring positions
- block_perm: int32 [12, 2], P('tensor'), may hold values from 0 to 1, each once within a row
- query_weight: bfloat16 [768, 768], P('dp', 'tensor'), may hold values from -0.21875 to 0.21875
- key_weight: bfloat16 [768, 768], P('dp', 'tensor'), may hold values from -0.21875 to 0.21875
- value_weight: bfloat16 [768, 768], P('dp', 'tensor'), may hold values from -0.21875 to 0.21875
- output_weight: bfloat16 [768, 768], P('tensor', 'dp'), may hold values from -4 to 4
- inner_weight: bfloat16 [768, 3072], P('dp', 'tensor'), may hold values from -0.21875 to 0.21875
- outer_weight: bfloat16 [3072, 768], P('tensor', 'dp'), may hold values from -0.109375 to 0.109375
- first_gain: bfloat16 [768], P(('dp', 'tensor')), may hold values from 0.5 to 1.5
- first_shift: bfloat16 [768], P(('dp', 'tensor')), may hold values from -3 to 3
- second_gain: bfloat16 [768], P(('dp', 'tensor')), may hold values from 0.5 to 1.5
- second_shift: bfloat16 [768], P(('dp', 'tensor')), may hold values from -3 to 3
Outputs:
- layer_out: bfloat16 [2, 16384, 768], P(None, ('dp', 'tensor'))
- input_grad: float32 [2, 16384, 768], P(None, ('dp', 'tensor'))
- grad_query: float32 [768, 768], P('dp', 'tensor')
- grad_key: float32 [768, 768], P('dp', 'tensor')
- grad_value: float32 [768, 768], P('dp', 'tensor')
- grad_output: float32 [768, 768], P('tensor', 'dp')
- grad_inner: float32 [768, 3072], P('dp', 'tensor')
- grad_outer: float32 [3072, 768], P('tensor', 'dp')
- grad_first_gain: float32 [768], P(('dp', 'tensor'))
- grad_first_shift: float32 [768], P(('dp', 'tensor'))
- grad_second_gain: float32 [768], P(('dp', 'tensor'))
- grad_second_shift: float32 [768], P(('dp', 'tensor'))
The draws below stay inside these ranges and needn't reach their ends.
Inputs may be any that keep to these rules, and one draw needn't show every extreme that they name: `seg_ids`: along a group's 512 continuation tokens the ids never fall; each of the 4 continuations holds 1 to 192 tokens, and one holds exactly 192. `block_perm`: each head's row names both prompt blocks, each once.
All inputs are finite; a program needn't handle non-finite values.
Results may differ from the reference program's by a relative error of at most 0.018.
Values may be sent and summed in bfloat16 or wider, within the bound.
A program may use at most 128 MiB of HBM per device.

```python
import math
import jax
import jax.numpy as jnp
import numpy as np
from jax import lax

D = 768
HEADS = 12
HEAD_WIDTH = 64
FF = 3072
PROMPT_LENGTH = 512
CONT_TOK = 512
CONT_SEGS = 4
MICRO = 2
CONT_MOST = 192
GROUP_TOK = 1024
GROUPS = 16
TOKENS = 16384


def with_spikes(result, key, source, target, blocks, factor):
    def block_of(dim):
        return (jnp.arange(result.shape[dim]) // (result.shape[dim] // blocks)).reshape((-1,) + (1,) * (result.ndim - 1 - dim))

    one_side = jax.random.permutation(key, blocks)[block_of(target)]
    second = (block_of(target) + blocks // 2) % blocks
    return jnp.where((block_of(source) == one_side) | (block_of(source) == second), factor * result, result)


def level_of(rng, dims, pieces, smallest, largest):
    factor_of = 1.0
    for axis_at, shards_of in pieces:
        steps = jax.random.uniform(jax.random.fold_in(jax.random.fold_in(rng, 6), axis_at), (shards_of,), jnp.float32, smallest / len(pieces), largest / len(pieces))
        factor_of = factor_of * jnp.repeat(jnp.exp(steps), dims[axis_at] // shards_of).reshape((-1,) + (1,) * (len(dims) - 1 - axis_at))
    return factor_of


def split_up(amount, total, reach, lean):
    portions = [(1 << 20) // math.isqrt(standing ** lean) + 1 for standing in range(2, amount + 1)]
    surplus, counts = total - reach - (amount - 1), [1] * (amount - 1)
    while surplus > 0:
        free = [i for i in range(amount - 1) if counts[i] < reach]
        whole, left = sum([portions[i] for i in free]), surplus
        for i in free:
            extra = min(reach - counts[i], max(1, left * portions[i] // whole), surplus)
            counts[i] = counts[i] + extra
            surplus = surplus - extra
    return np.array([reach] + counts)


def uneven_parts(key, number_of, total, limit, slope):
    if number_of == 2:
        one = jax.random.randint(key, (), max(1, total - limit), min(limit, total - 1) + 1)
        return jnp.stack([one, total - one])
    sizes = jnp.asarray(split_up(number_of, total, limit, slope), jnp.int32)
    pairs = (number_of - 1) // 2
    source_of, taker = sizes[1:1 + 2 * pairs:2], sizes[2:2 + 2 * pairs:2]
    margin = jnp.minimum(source_of - 1, limit - taker)
    shifted = jax.random.randint(jax.random.fold_in(key, 1), (pairs,), 0, 1 << 20) % (margin + 1)
    sizes = sizes.at[1:1 + 2 * pairs:2].set(source_of - shifted).at[2:2 + 2 * pairs:2].set(taker + shifted)
    return sizes[jax.random.permutation(jax.random.fold_in(key, 2), number_of)]


def normal_values(stream_key, shape, width, most, pieces=(), kind=jnp.bfloat16):
    gain = level_of(stream_key, shape, pieces, -0.22, 0.18) if pieces else 1.0
    drawn = jax.random.normal(stream_key, shape, jnp.float32) * width * gain
    return jnp.minimum(jnp.maximum(drawn, -most), most).astype(kind)


def gaussian_with(stream_key, extent, width, limit, split, heavy, dtype=jnp.bfloat16):
    entries = width * jax.random.normal(stream_key, extent, jnp.float32)
    if split:
        entries = entries * level_of(stream_key, extent, split, -0.22, 0.18)
    return jnp.clip(with_spikes(entries, jax.random.fold_in(stream_key, 3), *heavy), -limit, limit).astype(dtype)


def setup_inputs(seed: int = 0) -> dict:
    seeds = jax.random.split(jax.random.key(seed), 15)
    return {
        "inputs": gaussian_with(seeds[0], (MICRO, TOKENS, D), 1.0, 6.0, ((1, 32),), (1, 2, 32, 2.75)),
        "cotangent": gaussian_with(seeds[1], (MICRO, TOKENS, D), 1.0, 6.0, ((1, 32),), (1, 2, 32, 2.75)),
        "seg_ids": jax.vmap(lambda own: jnp.searchsorted(jnp.cumsum(uneven_parts(own, CONT_SEGS, CONT_TOK, CONT_MOST, 1)), jnp.arange(CONT_TOK), side="right"))(jax.random.split(seeds[2], MICRO * GROUPS)).reshape((MICRO, GROUPS, CONT_TOK)).astype(jnp.int32),
        "block_perm": jax.vmap(lambda own: jax.random.permutation(own, 2))(jax.random.split(seeds[3], HEADS)).reshape((HEADS, 2)).astype(jnp.int32),
        "query_weight": normal_values(seeds[4], (D, D), D ** -0.5, 0.21875, ((0, 16), (1, 2))),
        "key_weight": normal_values(seeds[5], (D, D), D ** -0.5, 0.21875, ((0, 16), (1, 2))),
        "value_weight": normal_values(seeds[6], (D, D), D ** -0.5, 0.21875, ((0, 16), (1, 2))),
        "output_weight": normal_values(seeds[7], (D, D), 2 ** -0.5, 4.0, ((0, 2), (1, 16))),
        "inner_weight": normal_values(seeds[8], (D, FF), D ** -0.5, 0.21875, ((0, 16), (1, 2))),
        "outer_weight": normal_values(seeds[9], (FF, D), FF ** -0.5, 0.109375, ((0, 2), (1, 16))),
        "first_gain": jnp.clip(1.0 + 0.1 * jax.random.normal(seeds[10], (D,), jnp.float32), 0.5, 1.5).astype(jnp.bfloat16),
        "first_shift": normal_values(seeds[11], (D,), 0.5, 3.0, ((0, 32),)),
        "second_gain": jnp.clip(1.0 + 0.1 * jax.random.normal(seeds[12], (D,), jnp.float32), 0.5, 1.5).astype(jnp.bfloat16),
        "second_shift": normal_values(seeds[13], (D,), 0.5, 3.0, ((0, 32),)),
    }


@jax.custom_vjp
def low(v):
    return lax.optimization_barrier(v.astype(jnp.bfloat16)).astype(jnp.float32)

@jax.custom_vjp
def lowered_backward(v):
    return v

def low_keep(v):
    return (low(v), None)

def low_pass(kept, grad):
    return (grad,)

def back_keep(v):
    return (v, None)

def back_low(kept, grad):
    return (low(grad),)
low.defvjp(low_keep, low_pass)
lowered_backward.defvjp(back_keep, back_low)
EPSILON = 1e-05
MASKED = -1e+30
ROOT_HALF = 1.0 / math.sqrt(2.0)
TOP_PRECISION = lax.Precision.HIGHEST

def product(left_matrix, right_matrix):
    return jnp.dot(left_matrix, right_matrix, precision=TOP_PRECISION, preferred_element_type=jnp.float32)

def normalize(residual, gain_vector, shift_vector):
    centred = residual - lax.optimization_barrier(jnp.mean(residual, axis=-1, keepdims=True))
    inverse = lax.rsqrt(lax.optimization_barrier(jnp.mean(centred * centred, axis=-1, keepdims=True)) + EPSILON)
    return centred * inverse * gain_vector + shift_vector

def softmax_rows(scores):
    weights_row = jnp.exp(scores - lax.optimization_barrier(jnp.max(scores, axis=-1, keepdims=True)))
    return weights_row / lax.optimization_barrier(jnp.sum(weights_row, axis=-1, keepdims=True))

def attend_head(query_rows, key_rows, value_rows, block_order, segments):
    softmax_factor = 1.0 / math.sqrt(HEAD_WIDTH)
    half_len = PROMPT_LENGTH // 2
    blocked_queries = query_rows[:PROMPT_LENGTH].reshape(2, half_len, HEAD_WIDTH)
    key_prompt = key_rows[:PROMPT_LENGTH].reshape(2, half_len, HEAD_WIDTH)
    value_prompt = value_rows[:PROMPT_LENGTH].reshape(2, half_len, HEAD_WIDTH)
    first_pick = (block_order == 0)[:, None, None]
    blocked_keys = jnp.where(first_pick, key_prompt[0][None], key_prompt[1][None])
    blocked_values = jnp.where(first_pick, value_prompt[0][None], value_prompt[1][None])
    prompt_score_rows = lowered_backward(jnp.einsum('jze,jce->jzc', blocked_queries, blocked_keys, precision=TOP_PRECISION) * softmax_factor)
    prompt_probabilities = low(softmax_rows(prompt_score_rows))
    prompt_output = jnp.einsum('tps,tsg->tpg', prompt_probabilities, blocked_values, precision=TOP_PRECISION).reshape(PROMPT_LENGTH, HEAD_WIDTH)
    key_segments = jnp.concatenate([jnp.full((PROMPT_LENGTH,), -1, jnp.int32), segments])
    key_mask = (key_segments[None, :] < 0) | (key_segments[None, :] == segments[:, None])
    suffix_scores = lowered_backward(product(query_rows[PROMPT_LENGTH:], key_rows.T) * softmax_factor)
    suffix_scores = jnp.where(key_mask, suffix_scores, MASKED)
    suffix_probs = low(softmax_rows(suffix_scores))
    suffix_out = product(suffix_probs, value_rows)
    return jnp.concatenate([prompt_output, suffix_out], axis=0)

def split_heads(rows_matrix):
    return rows_matrix.reshape(GROUP_TOK, HEADS, HEAD_WIDTH).transpose(1, 0, 2)

def layer(group_rows, segments, block_perm, query_weight, key_weight, value_weight, output_weight, inner_weight, outer_weight, first_gain, first_shift, second_gain, second_shift):
    query_rows = lowered_backward(low(product(group_rows, query_weight)))
    key_rows = lowered_backward(low(product(group_rows, key_weight)))
    value_rows = lowered_backward(low(product(group_rows, value_weight)))
    head_out = jax.vmap(attend_head, in_axes=(0, 0, 0, 0, None))(split_heads(query_rows), split_heads(key_rows), split_heads(value_rows), block_perm, segments)
    attended = lowered_backward(low(head_out.transpose(1, 0, 2).reshape(GROUP_TOK, D)))
    attention_sum = lowered_backward(product(attended, output_weight))
    hidden = normalize(group_rows + attention_sum, first_gain, first_shift)
    preactivation = lowered_backward(product(low(hidden), inner_weight))
    activated = low(0.5 * preactivation * (1.0 + lax.erf(preactivation * ROOT_HALF)))
    branch_out = lowered_backward(product(activated, outer_weight))
    return normalize(hidden + branch_out, second_gain, second_shift)

def reference(inputs, cotangent, seg_ids, block_perm, query_weight, key_weight, value_weight, output_weight, inner_weight, outer_weight, first_gain, first_shift, second_gain, second_shift):
    weights = tuple((matrix.astype(jnp.float32) for matrix in (query_weight, key_weight, value_weight, output_weight, inner_weight, outer_weight, first_gain, first_shift, second_gain, second_shift)))
    group_count = MICRO * GROUPS
    flat_inputs = inputs.reshape(group_count, GROUP_TOK, D)
    flat_cotangent = cotangent.reshape(group_count, GROUP_TOK, D)
    flat_segments = seg_ids.reshape(group_count, CONT_TOK)

    def one_group(totals, group_items):
        group_in, group_cot, segments = group_items

        def run_layer(group_rows, *params):
            return layer(group_rows, segments, block_perm, *params)
        outputs, pullback = jax.vjp(run_layer, group_in.astype(jnp.float32), *weights)
        gradients = pullback(group_cot.astype(jnp.float32))
        totals = tuple((total + gradient for total, gradient in zip(totals, gradients[1:])))
        return (totals, (outputs.astype(jnp.bfloat16), gradients[0]))
    start_totals = tuple((jnp.zeros(matrix.shape, jnp.float32) for matrix in weights))
    totals, (outputs, input_grads) = lax.scan(one_group, start_totals, (flat_inputs, flat_cotangent, flat_segments))
    return (outputs.reshape(MICRO, TOKENS, D), input_grads.reshape(MICRO, TOKENS, D), totals[0], totals[1], totals[2], totals[3], totals[4], totals[5], totals[6], totals[7], totals[8], totals[9])
```

```python
import functools
import math

import jax
import jax.numpy as jnp
from jax import lax
from jax.experimental import pallas as pl
from jax.experimental.pallas import tpu as pltpu
from jax.sharding import PartitionSpec as P

HEAD_WIDTH = 64
PROMPT_LENGTH = 512
CONT_TOK = 512
GROUP_TOK = PROMPT_LENGTH + CONT_TOK
HALF = PROMPT_LENGTH // 2
LANES = 2 * HEAD_WIDTH
CHUNK = 256

EPSILON = 1e-05
MASKED = -1e30
SCALE = 1.0 / math.sqrt(HEAD_WIDTH)
ROOT_HALF = 1.0 / math.sqrt(2.0)
ROOT_TWO_PI = 1.0 / math.sqrt(2.0 * math.pi)


BF = jnp.bfloat16
F32 = jnp.float32


def dot(left, right, dims):
    return lax.dot_general(left, right, (dims, ((), ())), preferred_element_type=F32)


def matmul(left, right):
    return dot(left, right, ((1,), (0,)))


def contract_rows(left, right):
    return dot(left, right, ((0,), (0,)))


def contract_cols(left, right):
    return dot(left, right, ((1,), (1,)))


def normalize(residual, gain_vector, shift_vector):
    centred = residual - jnp.mean(residual, axis=-1, keepdims=True)
    inverse = lax.rsqrt(jnp.mean(centred * centred, axis=-1, keepdims=True) + EPSILON)
    unit_rows = centred * inverse
    return (unit_rows * gain_vector + shift_vector, unit_rows, inverse)


def normalize_back(upstream, unit_rows, inverse, gain_vector):
    scaled = upstream * gain_vector
    first_mean = jnp.mean(scaled, axis=-1, keepdims=True)
    second_mean = jnp.mean(scaled * unit_rows, axis=-1, keepdims=True)
    return inverse * (scaled - first_mean - unit_rows * second_mean)


def gelu_pair(values):
    normal_cdf = 0.5 * (1.0 + lax.erf(values * ROOT_HALF))
    density = jnp.exp(-0.5 * values * values) * ROOT_TWO_PI
    return (values * normal_cdf, normal_cdf + values * density)


def head_lanes(head, value):
    lane = lax.broadcasted_iota(jnp.int32, value.shape, 1)
    return jnp.where((lane // HEAD_WIDTH) == head, value, jnp.zeros_like(value))


def forward_kernel(perm_ref, q_ref, k_ref, v_ref, bias_ref, out_ref, lse_ref, vt_ref, ot_ref):
    pair = pl.program_id(0)
    vt_ref[...] = v_ref[...].T
    for head in range(2):
        lanes = slice(head * HEAD_WIDTH, (head + 1) * HEAD_WIDTH)

        def finish(scores, values_t, columns):
            top = jnp.max(scores, axis=0, keepdims=True)
            weights = jnp.exp(scores - top)
            total = jnp.sum(weights, axis=0, keepdims=True)
            out_t = matmul(values_t, weights.astype(BF))
            ot_ref[lanes, columns] = out_t / total
            lse_ref[0, head : head + 1, columns] = top + jnp.log(total)

        for block in range(2):
            columns = slice(block * HALF, (block + 1) * HALF)
            start = pl.multiple_of(perm_ref[pair * 2 + head, block] * HALF, HALF)
            queries = head_lanes(head, q_ref[columns, :]) * SCALE
            scores = contract_cols(k_ref[pl.ds(start, HALF), :], queries.astype(BF))
            finish(scores, vt_ref[lanes, pl.ds(start, HALF)], columns)
        for chunk in range(CONT_TOK // CHUNK):
            first = PROMPT_LENGTH + chunk * CHUNK
            columns = slice(first, first + CHUNK)
            queries = (head_lanes(head, q_ref[columns, :]) * SCALE).astype(BF)
            scores = jnp.concatenate(
                [
                    contract_cols(k_ref[:PROMPT_LENGTH, :], queries),
                    contract_cols(k_ref[PROMPT_LENGTH:, :], queries)
                    + bias_ref[:, chunk * CHUNK : (chunk + 1) * CHUNK],
                ],
                axis=0,
            )
            finish(scores, vt_ref[lanes, :], columns)
    out_ref[...] = ot_ref[...].T.astype(BF)


def backward_kernel(
    perm_ref, q_ref, k_ref, v_ref, bias_ref, grad_ref, out_ref, lse_ref,
    dq_ref, dk_ref, dv_ref, kt_ref, dqt_ref, dka_ref, dva_ref, delta_ref,
):
    pair = pl.program_id(0)
    kt_ref[...] = k_ref[...].T
    product = (grad_ref[...].astype(F32) * out_ref[...].astype(F32)).T
    for head in range(2):
        lanes = slice(head * HEAD_WIDTH, (head + 1) * HEAD_WIDTH)
        delta_ref[head : head + 1, :] = jnp.sum(product[lanes, :], axis=0, keepdims=True)
    for head in range(2):
        lanes = slice(head * HEAD_WIDTH, (head + 1) * HEAD_WIDTH)

        def score_grad(scores, values, grads, columns):
            probs = jnp.exp(scores - lse_ref[0, head : head + 1, columns])
            prob_grad = contract_cols(values, grads)
            grad_scores = probs * (prob_grad - delta_ref[head : head + 1, columns])
            return probs.astype(BF), grad_scores.astype(BF)

        for chunk in range(CONT_TOK // CHUNK):
            first = PROMPT_LENGTH + chunk * CHUNK
            columns = slice(first, first + CHUNK)
            queries = (head_lanes(head, q_ref[columns, :]) * SCALE).astype(BF)
            grads = head_lanes(head, grad_ref[columns, :])
            scores = jnp.concatenate(
                [
                    contract_cols(k_ref[:PROMPT_LENGTH, :], queries),
                    contract_cols(k_ref[PROMPT_LENGTH:, :], queries)
                    + bias_ref[:, chunk * CHUNK : (chunk + 1) * CHUNK],
                ],
                axis=0,
            )
            probs, grad_scores = score_grad(scores, v_ref[...], grads, columns)
            dqt_ref[lanes, columns] = matmul(kt_ref[lanes, :], grad_scores) * SCALE
            key_part = matmul(grad_scores, queries)
            value_part = matmul(probs, grads)
            if head == 0 and chunk == 0:
                dka_ref[...] = key_part
                dva_ref[...] = value_part
            else:
                dka_ref[...] += key_part
                dva_ref[...] += value_part
        for block in range(2):
            columns = slice(block * HALF, (block + 1) * HALF)
            start = pl.multiple_of(perm_ref[pair * 2 + head, block] * HALF, HALF)
            picked = pl.ds(start, HALF)
            queries = (head_lanes(head, q_ref[columns, :]) * SCALE).astype(BF)
            grads = head_lanes(head, grad_ref[columns, :])
            scores = contract_cols(k_ref[picked, :], queries)
            probs, grad_scores = score_grad(scores, v_ref[picked, :], grads, columns)
            dqt_ref[lanes, columns] = matmul(kt_ref[lanes, picked], grad_scores) * SCALE
            dka_ref[picked, :] += matmul(grad_scores, queries)
            dva_ref[picked, :] += matmul(probs, grads)
    dq_ref[...] = dqt_ref[...].T.astype(BF)
    dk_ref[...] = dka_ref[...].astype(BF)
    dv_ref[...] = dva_ref[...].astype(BF)


VMEM_LIMIT = 56 * 1024 * 1024


def column_spec(offset):
    return pl.BlockSpec((GROUP_TOK, LANES), lambda i, offset=offset: (0, offset + i))


def bias_spec():
    return pl.BlockSpec((CONT_TOK, CONT_TOK), lambda i: (0, 0))


def lse_spec():
    return pl.BlockSpec((1, 8, GROUP_TOK), lambda i: (i, 0, 0))


def attention_forward(perm, qkv, bias):
    width = qkv.shape[1] // 3
    pairs = width // LANES
    return pl.pallas_call(
        forward_kernel,
        grid=(pairs,),
        in_specs=[
            pl.BlockSpec(memory_space=pltpu.SMEM),
            column_spec(0),
            column_spec(pairs),
            column_spec(2 * pairs),
            bias_spec(),
        ],
        out_specs=[column_spec(0), lse_spec()],
        out_shape=[
            jax.ShapeDtypeStruct((GROUP_TOK, width), BF),
            jax.ShapeDtypeStruct((pairs, 8, GROUP_TOK), F32),
        ],
        scratch_shapes=[
            pltpu.VMEM((LANES, GROUP_TOK), BF),
            pltpu.VMEM((LANES, GROUP_TOK), F32),
        ],
        compiler_params=pltpu.CompilerParams(vmem_limit_bytes=VMEM_LIMIT),
        cost_estimate=pl.CostEstimate(
            flops=pairs * 8 * 655360 * 256, bytes_accessed=4 * GROUP_TOK * width * 2, transcendentals=0
        ),
        name="attention_forward",
    )(perm, qkv, qkv, qkv, bias)


def attention_backward(perm, qkv, bias, grads, outs, lse):
    width = qkv.shape[1] // 3
    pairs = width // LANES
    return pl.pallas_call(
        backward_kernel,
        grid=(pairs,),
        in_specs=[
            pl.BlockSpec(memory_space=pltpu.SMEM),
            column_spec(0),
            column_spec(pairs),
            column_spec(2 * pairs),
            bias_spec(),
            column_spec(0),
            column_spec(0),
            lse_spec(),
        ],
        out_specs=[column_spec(0)] * 3,
        out_shape=[jax.ShapeDtypeStruct((GROUP_TOK, width), BF)] * 3,
        scratch_shapes=[
            pltpu.VMEM((LANES, GROUP_TOK), BF),
            pltpu.VMEM((LANES, GROUP_TOK), F32),
            pltpu.VMEM((GROUP_TOK, LANES), F32),
            pltpu.VMEM((GROUP_TOK, LANES), F32),
            pltpu.VMEM((8, GROUP_TOK), F32),
        ],
        compiler_params=pltpu.CompilerParams(vmem_limit_bytes=VMEM_LIMIT),
        cost_estimate=pl.CostEstimate(
            flops=pairs * 20 * 655360 * 256, bytes_accessed=8 * GROUP_TOK * width * 2, transcendentals=0
        ),
        name="attention_backward",
    )(perm, qkv, qkv, qkv, bias, grads, outs, lse)


def swap_pair(value):
    return lax.ppermute(value, "tensor", [(0, 1), (1, 0)])


def swap_bit(value, bit, size):
    return lax.ppermute(value, "dp", [(i, i ^ (1 << bit)) for i in range(size)])


def pick(stacked, index, axis=0):
    return lax.dynamic_index_in_dim(stacked, index, axis, keepdims=False)


def reduce_tree(own, other, order, size, last_type=F32):
    bits = size.bit_length() - 1
    me = lax.axis_index("dp")
    held = [value.reshape((2,) * bits + (value.shape[0] // size,) + value.shape[1:]) for value in (own, other)]
    left = list(range(bits - 1, -1, -1))
    for step, move in enumerate(order):
        kind = last_type if step == len(order) - 1 else own.dtype
        if move == "t":
            arrived = swap_pair(held[1])
            held = [(held[0].astype(F32) + arrived.astype(F32)).astype(kind)]
            continue
        axis = left.index(move)
        left.remove(move)
        mine = lax.rem(lax.div(me, 1 << move), 2)
        arrived = [swap_bit(pick(value, 1 - mine, axis), move, size) for value in held]
        held = [
            (pick(value, mine, axis).astype(F32) + got.astype(F32)).astype(kind)
            for value, got in zip(held, arrived)
        ]
    return held[0]


def tree_order(size, pair_first):
    bits = size.bit_length() - 1
    rest = list(range(bits - 1, 1, -1))
    if pair_first:
        return [0, "t", 1] + rest
    return [0, 1, "t"] + rest


def local(
    inputs,
    cotangent,
    seg_ids,
    block_perm,
    query_weight,
    key_weight,
    value_weight,
    output_weight,
    inner_weight,
    outer_weight,
    first_gain,
    first_shift,
    second_gain,
    second_shift,
    size,
):
    rank = lax.axis_index("tensor")
    at_first = rank == 0

    def gather(shard):
        return lax.all_gather(shard, ("tensor", "dp"), axis=0, tiled=False).reshape(
            (2, size * shard.shape[0]) + shard.shape[1:]
        )

    def both(stacked):
        return pick(stacked, rank), pick(stacked, 1 - rank)

    width = query_weight.shape[1]
    hidden_width = inner_weight.shape[1]
    slot = query_weight.shape[0]
    vectors = jnp.concatenate([first_gain, first_shift, second_gain, second_shift])
    per_vector = first_gain.shape[0]
    vector_block = jnp.pad(vectors[None, :], ((0, slot - 1), (0, 128 - vectors.shape[0])))
    w_qkv = gather(jnp.concatenate([query_weight, key_weight, value_weight], axis=1))
    w_mid = gather(jnp.concatenate([output_weight.T, vector_block, inner_weight], axis=1))
    w_last = gather(outer_weight.T)
    w_qkv = both(w_qkv)
    all_vectors = w_mid[:, :, width : width + 128].reshape(2, size, slot, 128)[:, :, 0, : 4 * per_vector]
    all_vectors = all_vectors.reshape(2, size, 4, per_vector).transpose(2, 1, 0, 3).reshape(4, -1)
    gain_one, shift_one, gain_two, shift_two = [all_vectors[i].astype(F32) for i in range(4)]
    w_mid = both(w_mid)
    w_output = [value[:, :width] for value in w_mid]
    w_inner = [value[:, width + 128 :] for value in w_mid]
    w_outer = both(w_last)

    def collect(mine_and_other):
        mine = pick(mine_and_other, rank)
        arrived = swap_pair(pick(mine_and_other, 1 - rank))
        return jnp.concatenate(
            [jnp.where(at_first, mine, arrived), jnp.where(at_first, arrived, mine)], axis=0
        )

    def spread(rows):
        halves = rows.reshape((2, rows.shape[0] // 2) + rows.shape[1:])
        mine = pick(halves, rank)
        arrived = swap_pair(pick(halves, 1 - rank).astype(BF)).astype(rows.dtype)
        return jnp.stack([jnp.where(at_first, mine, arrived), jnp.where(at_first, arrived, mine)])

    rows = collect(inputs)
    upstream = collect(cotangent).astype(F32)
    segments = pick(seg_ids, rank)[0]
    bias = jnp.where(segments[:, None] == segments[None, :], 0.0, MASKED).astype(F32)
    perms = (block_perm, swap_pair(block_perm))

    qkv = [matmul(rows, weight).astype(BF) for weight in w_qkv]
    attended, lse = zip(*[attention_forward(p, value, bias) for p, value in zip(perms, qkv)])
    attention_sum = contract_cols(attended[0], w_output[0]) + contract_cols(attended[1], w_output[1])
    hidden, unit_one, inverse_one = normalize(rows.astype(F32) + attention_sum, gain_one, shift_one)
    hidden_low = hidden.astype(BF)
    activated, slope = zip(*[gelu_pair(matmul(hidden_low, weight)) for weight in w_inner])
    activated = [value.astype(BF) for value in activated]
    slope = [value.astype(BF) for value in slope]
    branch = contract_cols(activated[0], w_outer[0]) + contract_cols(activated[1], w_outer[1])
    layer_out, unit_two, inverse_two = normalize(hidden + branch, gain_two, shift_two)
    layer_rows = spread(layer_out.astype(BF))

    second_back = normalize_back(upstream, unit_two, inverse_two, gain_two)
    branch_grad = second_back.astype(BF)
    grad_outer = reduce_tree(
        *[contract_rows(branch_grad, value).astype(BF) for value in activated], tree_order(size, True), size
    )
    pre_grad = [
        (matmul(branch_grad, weight) * part.astype(F32)).astype(BF) for weight, part in zip(w_outer, slope)
    ]
    grad_inner = reduce_tree(
        *[contract_rows(hidden_low, value).astype(BF) for value in pre_grad], tree_order(size, False), size
    )
    hidden_back = second_back + contract_cols(pre_grad[0], w_inner[0]) + contract_cols(pre_grad[1], w_inner[1])
    first_back = normalize_back(hidden_back, unit_one, inverse_one, gain_one)
    norm_terms = jnp.stack(
        [
            jnp.sum(hidden_back * unit_one, axis=0),
            jnp.sum(hidden_back, axis=0),
            jnp.sum(upstream * unit_two, axis=0),
            jnp.sum(upstream, axis=0),
        ]
    )
    by_shard = norm_terms.reshape(4, size, 2, per_vector).transpose(2, 1, 0, 3).reshape(2, size, 4, per_vector)
    norm_shards = reduce_tree(*both(by_shard), tree_order(size, True), size)
    norm_shards = norm_shards.reshape(4, per_vector)

    attention_grad = first_back.astype(BF)
    grad_output = reduce_tree(
        *[contract_rows(attention_grad, value).astype(BF) for value in attended], tree_order(size, True), size
    )
    attended_grad = [matmul(attention_grad, weight).astype(BF) for weight in w_output]
    head_grads = [
        attention_backward(p, value, bias, grad, out, total)
        for p, value, grad, out, total in zip(perms, qkv, attended_grad, attended, lse)
    ]
    grad_qkv = reduce_tree(
        *[
            jnp.concatenate([contract_rows(rows, value).astype(BF) for value in parts], axis=1)
            for parts in head_grads
        ],
        tree_order(size, False),
        size,
    )
    input_grad = first_back
    for parts, weight in zip(head_grads, w_qkv):
        for index, value in enumerate(parts):
            input_grad = input_grad + contract_cols(value, weight[:, index * width : (index + 1) * width])
    input_rows = spread(input_grad)
    grad_query, grad_key, grad_value = [grad_qkv[:, i * width : (i + 1) * width] for i in range(3)]
    return (
        layer_rows,
        input_rows,
        grad_query,
        grad_key,
        grad_value,
        grad_output.T,
        grad_inner,
        grad_outer.T,
        norm_shards[0],
        norm_shards[1],
        norm_shards[2],
        norm_shards[3],
    )


def solution(mesh):
    rows = P(None, ("dp", "tensor"), None)
    columns = P("dp", "tensor")
    flipped = P("tensor", "dp")
    vector = P(("dp", "tensor"))
    return jax.shard_map(
        functools.partial(local, size=mesh.shape["dp"]),
        mesh=mesh,
        in_specs=(
            rows, rows, P(None, "dp", None), P("tensor", None),
            columns, columns, columns, flipped, columns, flipped,
            vector, vector, vector, vector,
        ),
        out_specs=(
            rows, rows, columns, columns, columns, flipped, columns, flipped,
            vector, vector, vector, vector,
        ),
        check_vma=False,
    )
```

```python
import functools
import math

import jax
import jax.numpy as jnp
from jax import lax
from jax.experimental import pallas as pl
from jax.experimental.pallas import tpu as pltpu
from jax.sharding import PartitionSpec as P

HEAD_WIDTH = 64
PROMPT_LENGTH = 512
CONT_TOK = 512
GROUP_TOK = PROMPT_LENGTH + CONT_TOK
HALF = PROMPT_LENGTH // 2
LANES = 2 * HEAD_WIDTH
CHUNK = 256

EPSILON = 1e-05
MASKED = -1e30
SCALE = 1.0 / math.sqrt(HEAD_WIDTH)
ROOT_HALF = 1.0 / math.sqrt(2.0)
ROOT_TWO_PI = 1.0 / math.sqrt(2.0 * math.pi)


BF = jnp.bfloat16
F32 = jnp.float32


def dot(left, right, dims):
    return lax.dot_general(left, right, (dims, ((), ())), preferred_element_type=F32)


def matmul(left, right):
    return dot(left, right, ((1,), (0,)))


def contract_rows(left, right):
    return dot(left, right, ((0,), (0,)))


def contract_cols(left, right):
    return dot(left, right, ((1,), (1,)))


def normalize(residual, gain_vector, shift_vector):
    centred = residual - jnp.mean(residual, axis=-1, keepdims=True)
    inverse = lax.rsqrt(jnp.mean(centred * centred, axis=-1, keepdims=True) + EPSILON)
    unit_rows = centred * inverse
    return (unit_rows * gain_vector + shift_vector, unit_rows, inverse)


def normalize_back(upstream, unit_rows, inverse, gain_vector):
    scaled = upstream * gain_vector
    first_mean = jnp.mean(scaled, axis=-1, keepdims=True)
    second_mean = jnp.mean(scaled * unit_rows, axis=-1, keepdims=True)
    return inverse * (scaled - first_mean - unit_rows * second_mean)


def gelu_pair(values):
    normal_cdf = 0.5 * (1.0 + lax.erf(values * ROOT_HALF))
    density = jnp.exp(-0.5 * values * values) * ROOT_TWO_PI
    return (values * normal_cdf, normal_cdf + values * density)


def head_lanes(head, value):
    lane = lax.broadcasted_iota(jnp.int32, value.shape, 1)
    return jnp.where((lane // HEAD_WIDTH) == head, value, jnp.zeros_like(value))


def forward_kernel(perm_ref, q_ref, k_ref, v_ref, bias_ref, out_ref, lse_ref, vt_ref, ot_ref):
    pair = pl.program_id(0)
    vt_ref[...] = v_ref[...].T
    for head in range(2):
        lanes = slice(head * HEAD_WIDTH, (head + 1) * HEAD_WIDTH)

        def finish(scores, values_t, columns):
            top = jnp.max(scores, axis=0, keepdims=True)
            weights = jnp.exp(scores - top)
            total = jnp.sum(weights, axis=0, keepdims=True)
            out_t = matmul(values_t, weights.astype(BF))
            ot_ref[lanes, columns] = out_t / total
            lse_ref[0, head : head + 1, columns] = top + jnp.log(total)

        for block in range(2):
            columns = slice(block * HALF, (block + 1) * HALF)
            start = pl.multiple_of(perm_ref[pair * 2 + head, block] * HALF, HALF)
            queries = head_lanes(head, q_ref[columns, :]) * SCALE
            scores = contract_cols(k_ref[pl.ds(start, HALF), :], queries.astype(BF))
            finish(scores, vt_ref[lanes, pl.ds(start, HALF)], columns)
        for chunk in range(CONT_TOK // CHUNK):
            first = PROMPT_LENGTH + chunk * CHUNK
            columns = slice(first, first + CHUNK)
            queries = (head_lanes(head, q_ref[columns, :]) * SCALE).astype(BF)
            scores = jnp.concatenate(
                [
                    contract_cols(k_ref[:PROMPT_LENGTH, :], queries),
                    contract_cols(k_ref[PROMPT_LENGTH:, :], queries)
                    + bias_ref[:, chunk * CHUNK : (chunk + 1) * CHUNK],
                ],
                axis=0,
            )
            finish(scores, vt_ref[lanes, :], columns)
    out_ref[...] = ot_ref[...].T.astype(BF)


def backward_kernel(
    perm_ref, q_ref, k_ref, v_ref, bias_ref, grad_ref, out_ref, lse_ref,
    dq_ref, dk_ref, dv_ref, kt_ref, dqt_ref, dka_ref, dva_ref, delta_ref,
):
    pair = pl.program_id(0)
    kt_ref[...] = k_ref[...].T
    product = (grad_ref[...].astype(F32) * out_ref[...].astype(F32)).T
    for head in range(2):
        lanes = slice(head * HEAD_WIDTH, (head + 1) * HEAD_WIDTH)
        delta_ref[head : head + 1, :] = jnp.sum(product[lanes, :], axis=0, keepdims=True)
    for head in range(2):
        lanes = slice(head * HEAD_WIDTH, (head + 1) * HEAD_WIDTH)

        def score_grad(scores, values, grads, columns):
            probs = jnp.exp(scores - lse_ref[0, head : head + 1, columns])
            prob_grad = contract_cols(values, grads)
            grad_scores = probs * (prob_grad - delta_ref[head : head + 1, columns])
            return probs.astype(BF), grad_scores.astype(BF)

        for chunk in range(CONT_TOK // CHUNK):
            first = PROMPT_LENGTH + chunk * CHUNK
            columns = slice(first, first + CHUNK)
            queries = (head_lanes(head, q_ref[columns, :]) * SCALE).astype(BF)
            grads = head_lanes(head, grad_ref[columns, :])
            scores = jnp.concatenate(
                [
                    contract_cols(k_ref[:PROMPT_LENGTH, :], queries),
                    contract_cols(k_ref[PROMPT_LENGTH:, :], queries)
                    + bias_ref[:, chunk * CHUNK : (chunk + 1) * CHUNK],
                ],
                axis=0,
            )
            probs, grad_scores = score_grad(scores, v_ref[...], grads, columns)
            dqt_ref[lanes, columns] = matmul(kt_ref[lanes, :], grad_scores) * SCALE
            key_part = matmul(grad_scores, queries)
            value_part = matmul(probs, grads)
            if head == 0 and chunk == 0:
                dka_ref[...] = key_part
                dva_ref[...] = value_part
            else:
                dka_ref[...] += key_part
                dva_ref[...] += value_part
        for block in range(2):
            columns = slice(block * HALF, (block + 1) * HALF)
            start = pl.multiple_of(perm_ref[pair * 2 + head, block] * HALF, HALF)
            picked = pl.ds(start, HALF)
            queries = (head_lanes(head, q_ref[columns, :]) * SCALE).astype(BF)
            grads = head_lanes(head, grad_ref[columns, :])
            scores = contract_cols(k_ref[picked, :], queries)
            probs, grad_scores = score_grad(scores, v_ref[picked, :], grads, columns)
            dqt_ref[lanes, columns] = matmul(kt_ref[lanes, picked], grad_scores) * SCALE
            dka_ref[picked, :] += matmul(grad_scores, queries)
            dva_ref[picked, :] += matmul(probs, grads)
    dq_ref[...] = dqt_ref[...].T.astype(BF)
    dk_ref[...] = dka_ref[...].astype(BF)
    dv_ref[...] = dva_ref[...].astype(BF)


GATHER_CUT = 1152
REDUCE_CUT = 1280
VMEM_LIMIT = 56 * 1024 * 1024


def column_spec(offset):
    return pl.BlockSpec((GROUP_TOK, LANES), lambda i, offset=offset: (0, offset + i))


def bias_spec():
    return pl.BlockSpec((CONT_TOK, CONT_TOK), lambda i: (0, 0))


def lse_spec():
    return pl.BlockSpec((1, 8, GROUP_TOK), lambda i: (i, 0, 0))


def attention_forward(perm, qkv, bias):
    width = qkv.shape[1] // 3
    pairs = width // LANES
    return pl.pallas_call(
        forward_kernel,
        grid=(pairs,),
        in_specs=[
            pl.BlockSpec(memory_space=pltpu.SMEM),
            column_spec(0),
            column_spec(pairs),
            column_spec(2 * pairs),
            bias_spec(),
        ],
        out_specs=[column_spec(0), lse_spec()],
        out_shape=[
            jax.ShapeDtypeStruct((GROUP_TOK, width), BF),
            jax.ShapeDtypeStruct((pairs, 8, GROUP_TOK), F32),
        ],
        scratch_shapes=[
            pltpu.VMEM((LANES, GROUP_TOK), BF),
            pltpu.VMEM((LANES, GROUP_TOK), F32),
        ],
        compiler_params=pltpu.CompilerParams(vmem_limit_bytes=VMEM_LIMIT),
        cost_estimate=pl.CostEstimate(
            flops=pairs * 8 * 655360 * 256, bytes_accessed=4 * GROUP_TOK * width * 2, transcendentals=0
        ),
        name="attention_forward",
    )(perm, qkv, qkv, qkv, bias)


def attention_backward(perm, qkv, bias, grads, outs, lse):
    width = qkv.shape[1] // 3
    pairs = width // LANES
    return pl.pallas_call(
        backward_kernel,
        grid=(pairs,),
        in_specs=[
            pl.BlockSpec(memory_space=pltpu.SMEM),
            column_spec(0),
            column_spec(pairs),
            column_spec(2 * pairs),
            bias_spec(),
            column_spec(0),
            column_spec(0),
            lse_spec(),
        ],
        out_specs=[column_spec(0)] * 3,
        out_shape=[jax.ShapeDtypeStruct((GROUP_TOK, width), BF)] * 3,
        scratch_shapes=[
            pltpu.VMEM((LANES, GROUP_TOK), BF),
            pltpu.VMEM((LANES, GROUP_TOK), F32),
            pltpu.VMEM((GROUP_TOK, LANES), F32),
            pltpu.VMEM((GROUP_TOK, LANES), F32),
            pltpu.VMEM((8, GROUP_TOK), F32),
        ],
        compiler_params=pltpu.CompilerParams(vmem_limit_bytes=VMEM_LIMIT),
        cost_estimate=pl.CostEstimate(
            flops=pairs * 20 * 655360 * 256, bytes_accessed=8 * GROUP_TOK * width * 2, transcendentals=0
        ),
        name="attention_backward",
    )(perm, qkv, qkv, qkv, bias, grads, outs, lse)


def gather_kernel(
    size, cut, shard_ref, inputs_ref, own_ref, other_ref, arrived_ref,
    local_sem, swap_sem, z_sem, y_sem, x_sem, near_sem, far_sem, core_sem,
):
    depth = size // 4
    me = lax.axis_index("dp")
    rank = lax.axis_index("tensor")
    z = lax.div(me, 4)
    y = lax.rem(lax.div(me, 2), 2)
    core = lax.rem(me, 2)

    def place(zz, yy, cc):
        return zz * 4 + yy * 2 + cc

    up = {"dp": place(lax.rem(z + 1, depth), y, core)}
    down = {"dp": place(lax.rem(z + depth - 1, depth), y, core)}
    side = {"dp": place(z, 1 - y, core)}
    twin = {"dp": place(z, y, 1 - core)}
    across = {"tensor": 1 - rank}

    barrier = pltpu.get_barrier_semaphore()
    for target in (up, down, side, twin, across):
        pl.semaphore_signal(barrier, inc=1, device_id=target, device_id_type=pl.DeviceIdType.MESH)
    pl.semaphore_wait(barrier, 5)

    started = []

    def send(source, landing, sems, target):
        copy = pltpu.make_async_remote_copy(
            src_ref=source,
            dst_ref=landing,
            send_sem=sems.at[0],
            recv_sem=sems.at[1],
            device_id=target,
            device_id_type=pl.DeviceIdType.MESH,
        )
        copy.start()
        started.append(copy)

    def receive(landing, sems, target):
        pltpu.make_async_remote_copy(
            src_ref=landing,
            dst_ref=landing,
            send_sem=sems.at[0],
            recv_sem=sems.at[1],
            device_id=target,
            device_id_type=pl.DeviceIdType.MESH,
        ).wait_recv()

    keep = pltpu.make_async_copy(shard_ref, own_ref.at[me], local_sem)
    keep.start()

    def slots(age):
        zz = lax.rem(z - age + depth, depth)
        return place(zz, y, core), place(zz, 1 - y, core)

    first = slice(0, cut)
    rest = slice(cut, shard_ref.shape[1])
    for step in range(depth + 2):
        if step < depth:
            mine, _ = slots(step)
            if step == 0:
                block = shard_ref
            else:
                block = own_ref.at[mine]
                receive(block, z_sem.at[step - 1], up)
            if step < depth - 1:
                send(block, own_ref.at[mine], z_sem.at[step], up)
            send(block, own_ref.at[mine], y_sem.at[step], side)
            send(block, other_ref.at[mine], x_sem.at[step], across)
            send(block, own_ref.at[mine], core_sem.at[0, step], twin)
            if step == 0:
                send(inputs_ref.at[1 - rank], arrived_ref, swap_sem, across)
        if 1 <= step <= depth:
            age = step - 1
            mine, beside = slots(age)
            receive(own_ref.at[beside], y_sem.at[age], side)
            send(own_ref.at[beside, :, first], other_ref.at[beside, :, first], near_sem.at[age], across)
            send(own_ref.at[beside], own_ref.at[beside], core_sem.at[1, age], twin)
            receive(other_ref.at[mine], x_sem.at[age], across)
            send(other_ref.at[mine, :, rest], other_ref.at[mine, :, rest], far_sem.at[age], side)
            send(other_ref.at[mine], other_ref.at[mine], core_sem.at[2, age], twin)
        if step >= 2:
            age = step - 2
            _, beside = slots(age)
            receive(other_ref.at[beside, :, first], near_sem.at[age], across)
            receive(other_ref.at[beside, :, rest], far_sem.at[age], side)
            send(other_ref.at[beside], other_ref.at[beside], core_sem.at[3, age], twin)
    receive(arrived_ref, swap_sem, across)
    for age in range(depth):
        zz = lax.rem(z - age + depth, depth)
        here, there = place(zz, y, 1 - core), place(zz, 1 - y, 1 - core)
        receive(own_ref.at[here], core_sem.at[0, age], twin)
        receive(own_ref.at[there], core_sem.at[1, age], twin)
        receive(other_ref.at[here], core_sem.at[2, age], twin)
        receive(other_ref.at[there], core_sem.at[3, age], twin)
    for copy in started:
        copy.wait_send()
    keep.wait()


def gather_weights(shard, inputs, size, cut):
    depth = size // 4
    whole = jax.ShapeDtypeStruct((size,) + shard.shape, shard.dtype)
    sems = pltpu.SemaphoreType.DMA
    return pl.pallas_call(
        functools.partial(gather_kernel, size, cut),
        in_specs=[pl.BlockSpec(memory_space=pl.ANY)] * 2,
        out_specs=[pl.BlockSpec(memory_space=pl.ANY)] * 3,
        out_shape=[whole, whole, jax.ShapeDtypeStruct(inputs.shape[1:], inputs.dtype)],
        scratch_shapes=[
            sems,
            sems((2,)),
            sems((depth - 1, 2)),
            sems((depth, 2)),
            sems((depth, 2)),
            sems((depth, 2)),
            sems((depth, 2)),
            sems((4, depth, 2)),
        ],
        compiler_params=pltpu.CompilerParams(collective_id=0, has_side_effects=True),
        name="gather_weights",
    )(shard, inputs)


def reduce_kernel(size, cut, widths, *refs):
    pieces = len(widths)
    parts = (refs[:pieces], refs[pieces : 2 * pieces])
    (
        rows_ref, total_ref, arrived_ref, held, got_core, got_near, got_far, got_y, got_x, got_z,
        load_sem, core_sem, swap_sem, near_sem, far_sem, y_sem, x_sem, z_sem,
    ) = refs[2 * pieces :]
    depth = size // 4
    me = lax.axis_index("dp")
    rank = lax.axis_index("tensor")
    z = lax.div(me, 4)
    y = lax.rem(lax.div(me, 2), 2)
    core = lax.rem(me, 2)

    def place(zz, yy, cc):
        return zz * 4 + yy * 2 + cc

    up = {"dp": place(lax.rem(z + 1, depth), y, core)}
    down = {"dp": place(lax.rem(z + depth - 1, depth), y, core)}
    side = {"dp": place(z, 1 - y, core)}
    twin = {"dp": place(z, y, 1 - core)}
    across = {"tensor": 1 - rank}

    barrier = pltpu.get_barrier_semaphore()
    for target in (up, down, side, twin, across):
        pl.semaphore_signal(barrier, inc=1, device_id=target, device_id_type=pl.DeviceIdType.MESH)
    pl.semaphore_wait(barrier, 5)

    started = []

    def send(source, landing, sems, target):
        copy = pltpu.make_async_remote_copy(
            src_ref=source,
            dst_ref=landing,
            send_sem=sems.at[0],
            recv_sem=sems.at[1],
            device_id=target,
            device_id_type=pl.DeviceIdType.MESH,
        )
        copy.start()
        started.append(copy)
        return copy

    def add(target, addend, columns=slice(None)):
        def rows_of(index, carry):
            at = pl.ds(pl.multiple_of(index * 16, 16), 16)
            target[at, columns] = (target[at, columns].astype(F32) + addend[at, :].astype(F32)).astype(BF)
            return carry

        lax.fori_loop(0, target.shape[0] // 16, rows_of, 0)

    waiting = {}
    for age in range(depth):
        zz = lax.rem(z + 2 * depth - 1 - age, depth)
        for beside in (1, 0):
            yy = 1 - y if beside else y
            for slot in (1, 0):
                loads = []
                low = 0
                for index, width in enumerate(widths):
                    columns = slice(low, low + width)
                    low += width
                    source = parts[slot][index]
                    passed = send(
                        source.at[place(zz, yy, 1 - core)],
                        got_core.at[slot, age, beside, :, columns],
                        core_sem.at[slot, age, beside, index],
                        twin,
                    )
                    load = pltpu.make_async_copy(
                        source.at[place(zz, yy, core)],
                        held.at[slot, age, beside, :, columns],
                        load_sem.at[slot, age, beside, index],
                    )
                    load.start()
                    loads.append((load, passed))
                waiting[slot, age, beside] = loads
    swapped = send(rows_ref, arrived_ref, swap_sem, across)

    first = slice(0, cut)
    rest = slice(cut, sum(widths))
    near, far, over_y, over_x, over_z = {}, {}, {}, {}, {}
    for step in range(depth + 2):
        if step < depth:
            age = step
            for beside in (1, 0):
                for slot in (1, 0):
                    for load, passed in waiting[slot, age, beside]:
                        load.wait()
                        passed.wait_recv()
                    add(held.at[slot, age, beside], got_core.at[slot, age, beside])
                    if beside and slot:
                        corner = held.at[1, age, 1]
                        near[age] = send(corner.at[:, first], got_near.at[age], near_sem.at[age], across)
                        far[age] = send(corner.at[:, rest], got_far.at[age], far_sem.at[age], side)
        if 1 <= step <= depth:
            age = step - 1
            near[age].wait_recv()
            add(held.at[0, age, 1], got_near.at[age], first)
            over_y[age] = send(held.at[0, age, 1], got_y.at[age], y_sem.at[age], side)
            far[age].wait_recv()
            add(held.at[1, age, 0], got_far.at[age], rest)
            over_x[age] = send(held.at[1, age, 0], got_x.at[age], x_sem.at[age], across)
        if step >= 2:
            age = step - 2
            over_y[age].wait_recv()
            over_x[age].wait_recv()
            if age:
                over_z[age - 1].wait_recv()

            def rows_of(index, carry, age=age):
                at = pl.ds(pl.multiple_of(index * 16, 16), 16)
                value = held[0, age, 0, at, :].astype(F32) + got_y[age, at, :].astype(F32)
                value = value + got_x[age, at, :].astype(F32)
                if age:
                    value = value + got_z[age - 1, at, :].astype(F32)
                if age < depth - 1:
                    held[0, age, 0, at, :] = value.astype(BF)
                else:
                    total_ref[at, :] = value
                return carry

            lax.fori_loop(0, total_ref.shape[0] // 16, rows_of, 0)
            if age < depth - 1:
                over_z[age] = send(held.at[0, age, 0], got_z.at[age], z_sem.at[age], up)
    swapped.wait_recv()
    for copy in started:
        copy.wait_send()


def reduce_blocks(own, other, rows, size, cut):
    depth = size // 4
    slot = own[0].shape[0] // size
    widths = tuple(value.shape[1] for value in own)
    wide = sum(widths)
    sems = pltpu.SemaphoreType.DMA
    blocks = [value.reshape(size, slot, value.shape[1]) for value in (*own, *other)]
    any_spec = pl.BlockSpec(memory_space=pl.ANY)
    return pl.pallas_call(
        functools.partial(reduce_kernel, size, cut, widths),
        in_specs=[any_spec] * (len(blocks) + 1),
        out_specs=[pl.BlockSpec(memory_space=pltpu.VMEM), any_spec],
        out_shape=[jax.ShapeDtypeStruct((slot, wide), F32), jax.ShapeDtypeStruct(rows.shape, rows.dtype)],
        scratch_shapes=[
            pltpu.VMEM((2, depth, 2, slot, wide), BF),
            pltpu.VMEM((2, depth, 2, slot, wide), BF),
            pltpu.VMEM((depth, slot, cut), BF),
            pltpu.VMEM((depth, slot, wide - cut), BF),
            pltpu.VMEM((depth, slot, wide), BF),
            pltpu.VMEM((depth, slot, wide), BF),
            pltpu.VMEM((depth - 1, slot, wide), BF),
            sems((2, depth, 2, len(widths))),
            sems((2, depth, 2, len(widths), 2)),
            sems((2,)),
            sems((depth, 2)),
            sems((depth, 2)),
            sems((depth, 2)),
            sems((depth, 2)),
            sems((depth - 1, 2)),
        ],
        compiler_params=pltpu.CompilerParams(
            collective_id=1, has_side_effects=True, vmem_limit_bytes=VMEM_LIMIT
        ),
        name="reduce_blocks",
    )(*blocks, rows)


def swap_pair(value):
    return lax.ppermute(value, "tensor", [(0, 1), (1, 0)])


def swap_bit(value, bit, size):
    return lax.ppermute(value, "dp", [(i, i ^ (1 << bit)) for i in range(size)])


def pick(stacked, index, axis=0):
    return lax.dynamic_index_in_dim(stacked, index, axis, keepdims=False)


def reduce_tree(own, other, order, size, last_type=F32):
    bits = size.bit_length() - 1
    me = lax.axis_index("dp")
    held = [value.reshape((2,) * bits + (value.shape[0] // size,) + value.shape[1:]) for value in (own, other)]
    left = list(range(bits - 1, -1, -1))
    for step, move in enumerate(order):
        kind = last_type if step == len(order) - 1 else own.dtype
        if move == "t":
            arrived = swap_pair(held[1])
            held = [(held[0].astype(F32) + arrived.astype(F32)).astype(kind)]
            continue
        axis = left.index(move)
        left.remove(move)
        mine = lax.rem(lax.div(me, 1 << move), 2)
        arrived = [swap_bit(pick(value, 1 - mine, axis), move, size) for value in held]
        held = [
            (pick(value, mine, axis).astype(F32) + got.astype(F32)).astype(kind)
            for value, got in zip(held, arrived)
        ]
    return held[0]


def tree_order(size, pair_first):
    bits = size.bit_length() - 1
    rest = list(range(bits - 1, 1, -1))
    if pair_first:
        return [0, "t", 1] + rest
    return [0, 1, "t"] + rest


def local(
    inputs,
    cotangent,
    seg_ids,
    block_perm,
    query_weight,
    key_weight,
    value_weight,
    output_weight,
    inner_weight,
    outer_weight,
    first_gain,
    first_shift,
    second_gain,
    second_shift,
    size,
):
    rank = lax.axis_index("tensor")
    at_first = rank == 0

    def both(stacked):
        return pick(stacked, rank), pick(stacked, 1 - rank)

    width = query_weight.shape[1]
    hidden_width = inner_weight.shape[1]
    slot = query_weight.shape[0]
    vectors = jnp.concatenate([first_gain, first_shift, second_gain, second_shift])
    per_vector = first_gain.shape[0]
    vector_block = jnp.pad(vectors[None, :], ((0, slot - 1), (0, 128 - vectors.shape[0])))
    shard = jnp.concatenate(
        [query_weight, key_weight, value_weight, output_weight.T, vector_block, inner_weight, outer_weight.T], axis=1
    )
    own, other, arrived_rows = gather_weights(shard, inputs, size, GATHER_CUT)
    flat = [value.reshape(-1, value.shape[-1]) for value in (own, other)]
    edges = [0, 3 * width, 4 * width, 4 * width + 128, 4 * width + 128 + hidden_width, shard.shape[1]]
    w_qkv, w_output, vector_rows, w_inner, w_outer = [
        [value[:, low:high] for value in flat] for low, high in zip(edges[:-1], edges[1:])
    ]
    vector_rows = [value.reshape(size, slot, 128)[:, 0, : 4 * per_vector] for value in vector_rows]
    all_vectors = jnp.stack(
        [jnp.where(at_first, *vector_rows), jnp.where(at_first, *vector_rows[::-1])], axis=1
    )
    all_vectors = all_vectors.reshape(size, 2, 4, per_vector).transpose(2, 0, 1, 3).reshape(4, -1)
    gain_one, shift_one, gain_two, shift_two = [all_vectors[i].astype(F32) for i in range(4)]

    def collect(mine_and_other, arrived):
        mine = pick(mine_and_other, rank)
        return jnp.concatenate(
            [jnp.where(at_first, mine, arrived), jnp.where(at_first, arrived, mine)], axis=0
        )

    def spread(rows, arrived=None):
        halves = rows.reshape((2, rows.shape[0] // 2) + rows.shape[1:])
        mine = pick(halves, rank)
        if arrived is None:
            arrived = swap_pair(pick(halves, 1 - rank).astype(BF))
        arrived = arrived.astype(rows.dtype)
        return jnp.stack([jnp.where(at_first, mine, arrived), jnp.where(at_first, arrived, mine)])

    rows = collect(inputs, arrived_rows)
    arrived_rows, late = lax.optimization_barrier((arrived_rows, pick(cotangent, 1 - rank)))
    upstream = collect(cotangent, swap_pair(late)).astype(F32)
    segments = pick(seg_ids, rank)[0]
    bias = jnp.where(segments[:, None] == segments[None, :], 0.0, MASKED).astype(F32)
    perms = (block_perm, swap_pair(block_perm))

    qkv = [matmul(rows, weight).astype(BF) for weight in w_qkv]
    attended, lse = zip(*[attention_forward(p, value, bias) for p, value in zip(perms, qkv)])
    attention_sum = contract_cols(attended[0], w_output[0]) + contract_cols(attended[1], w_output[1])
    hidden, unit_one, inverse_one = normalize(rows.astype(F32) + attention_sum, gain_one, shift_one)
    hidden_low = hidden.astype(BF)
    activated, slope = zip(*[gelu_pair(matmul(hidden_low, weight)) for weight in w_inner])
    activated = [value.astype(BF) for value in activated]
    slope = [value.astype(BF) for value in slope]
    branch = contract_cols(activated[0], w_outer[0]) + contract_cols(activated[1], w_outer[1])
    layer_out, unit_two, inverse_two = normalize(hidden + branch, gain_two, shift_two)
    layer_rows = spread(layer_out.astype(BF))

    second_back = normalize_back(upstream, unit_two, inverse_two, gain_two)
    branch_grad = second_back.astype(BF)
    outer_terms = [contract_rows(branch_grad, value).astype(BF) for value in activated]
    pre_grad = [
        (matmul(branch_grad, weight) * part.astype(F32)).astype(BF) for weight, part in zip(w_outer, slope)
    ]
    inner_terms = [contract_rows(hidden_low, value).astype(BF) for value in pre_grad]
    hidden_back = second_back + contract_cols(pre_grad[0], w_inner[0]) + contract_cols(pre_grad[1], w_inner[1])
    first_back = normalize_back(hidden_back, unit_one, inverse_one, gain_one)
    norm_terms = jnp.stack(
        [
            jnp.sum(hidden_back * unit_one, axis=0),
            jnp.sum(hidden_back, axis=0),
            jnp.sum(upstream * unit_two, axis=0),
            jnp.sum(upstream, axis=0),
        ]
    )
    by_shard = norm_terms.reshape(4, size, 2, per_vector).transpose(2, 1, 0, 3).reshape(2, size, 4, per_vector)
    vector_terms = [
        jnp.pad(value.reshape(size, 1, 4 * per_vector), ((0, 0), (0, slot - 1), (0, 128 - 4 * per_vector)))
        .reshape(size * slot, 128)
        .astype(BF)
        for value in both(by_shard)
    ]

    attention_grad = first_back.astype(BF)
    output_terms = [contract_rows(attention_grad, value).astype(BF) for value in attended]
    attended_grad = [matmul(attention_grad, weight).astype(BF) for weight in w_output]
    head_grads = [
        attention_backward(p, value, bias, grad, out, total)
        for p, value, grad, out, total in zip(perms, qkv, attended_grad, attended, lse)
    ]
    head_terms = [
        [contract_rows(rows, value).astype(BF) for value in parts] for parts in head_grads
    ]
    input_grad = first_back
    for parts, weight in zip(head_grads, w_qkv):
        for index, value in enumerate(parts):
            input_grad = input_grad + contract_cols(value, weight[:, index * width : (index + 1) * width])
    terms = [
        (outer, inner, output, vector, *heads)
        for outer, inner, output, vector, heads in zip(
            outer_terms, inner_terms, output_terms, vector_terms, head_terms
        )
    ]
    if size == 16:
        half = GROUP_TOK // 2
        leaving = pick(input_grad.reshape(2, half, -1), 1 - rank).astype(BF)
        total, arrived = reduce_blocks(*terms, leaving, size, REDUCE_CUT)
    else:
        packed = [jnp.concatenate(value, axis=1) for value in terms]
        total, arrived = reduce_tree(*packed, tree_order(size, True), size), None
        total = total.reshape(slot, -1)
    input_rows = spread(input_grad, arrived)
    edges = [0, hidden_width, 2 * hidden_width, 2 * hidden_width + width, 2 * hidden_width + width + 128]
    edges += [edges[-1] + (i + 1) * width for i in range(3)]
    grad_outer, grad_inner, grad_output, norm_rows, grad_query, grad_key, grad_value = [
        total[:, low:high] for low, high in zip(edges[:-1], edges[1:])
    ]
    norm_shards = norm_rows[0, : 4 * per_vector].reshape(4, per_vector)
    return (
        layer_rows,
        input_rows,
        grad_query,
        grad_key,
        grad_value,
        grad_output.T,
        grad_inner,
        grad_outer.T,
        norm_shards[0],
        norm_shards[1],
        norm_shards[2],
        norm_shards[3],
    )


def solution(mesh):
    rows = P(None, ("dp", "tensor"), None)
    columns = P("dp", "tensor")
    flipped = P("tensor", "dp")
    vector = P(("dp", "tensor"))
    return jax.shard_map(
        functools.partial(local, size=mesh.shape["dp"]),
        mesh=mesh,
        in_specs=(
            rows, rows, P(None, "dp", None), P("tensor", None),
            columns, columns, columns, flipped, columns, flipped,
            vector, vector, vector, vector,
        ),
        out_specs=(
            rows, rows, columns, columns, columns, flipped, columns, flipped,
            vector, vector, vector, vector,
        ),
        check_vma=False,
    )
```

```python
import functools
import math

import jax
import jax.numpy as jnp
from jax import lax
from jax.experimental import pallas as pl
from jax.experimental.pallas import tpu as pltpu
from jax.sharding import PartitionSpec as P

HEAD_WIDTH = 64
PROMPT_LENGTH = 512
CONT_TOK = 512
GROUP_TOK = PROMPT_LENGTH + CONT_TOK
HALF = PROMPT_LENGTH // 2
LANES = 2 * HEAD_WIDTH
CHUNK = 256

EPSILON = 1e-05
MASKED = -1e30
SCALE = 1.0 / math.sqrt(HEAD_WIDTH)
ROOT_HALF = 1.0 / math.sqrt(2.0)
ROOT_TWO_PI = 1.0 / math.sqrt(2.0 * math.pi)


BF = jnp.bfloat16
F32 = jnp.float32


def dot(left, right, dims):
    return lax.dot_general(left, right, (dims, ((), ())), preferred_element_type=F32)


def matmul(left, right):
    return dot(left, right, ((1,), (0,)))


def contract_rows(left, right):
    return dot(left, right, ((0,), (0,)))


def contract_cols(left, right):
    return dot(left, right, ((1,), (1,)))


def normalize(residual, gain_vector, shift_vector):
    centred = residual - jnp.mean(residual, axis=-1, keepdims=True)
    inverse = lax.rsqrt(jnp.mean(centred * centred, axis=-1, keepdims=True) + EPSILON)
    unit_rows = centred * inverse
    return (unit_rows * gain_vector + shift_vector, unit_rows, inverse)


def normalize_back(upstream, unit_rows, inverse, gain_vector):
    scaled = upstream * gain_vector
    first_mean = jnp.mean(scaled, axis=-1, keepdims=True)
    second_mean = jnp.mean(scaled * unit_rows, axis=-1, keepdims=True)
    return inverse * (scaled - first_mean - unit_rows * second_mean)


def gelu_pair(values):
    normal_cdf = 0.5 * (1.0 + lax.erf(values * ROOT_HALF))
    density = jnp.exp(-0.5 * values * values) * ROOT_TWO_PI
    return (values * normal_cdf, normal_cdf + values * density)


def head_lanes(head, value):
    lane = lax.broadcasted_iota(jnp.int32, value.shape, 1)
    return jnp.where((lane // HEAD_WIDTH) == head, value, jnp.zeros_like(value))


def thirds(ref):
    return [ref.at[:, i * LANES : (i + 1) * LANES] for i in range(3)]


def forward_kernel(perm_ref, qkv_ref, bias_ref, out_ref, lse_ref, vt_ref, ot_ref):
    pair = pl.program_id(0)
    q_ref, k_ref, v_ref = thirds(qkv_ref)
    vt_ref[...] = v_ref[...].T
    for head in range(2):
        lanes = slice(head * HEAD_WIDTH, (head + 1) * HEAD_WIDTH)

        def finish(scores, values_t, columns):
            top = jnp.max(scores, axis=0, keepdims=True)
            weights = jnp.exp(scores - top)
            total = jnp.sum(weights, axis=0, keepdims=True)
            out_t = matmul(values_t, weights.astype(BF))
            ot_ref[lanes, columns] = out_t / total
            lse_ref[0, head : head + 1, columns] = top + jnp.log(total)

        for block in range(2):
            columns = slice(block * HALF, (block + 1) * HALF)
            start = pl.multiple_of(perm_ref[pair * 2 + head, block] * HALF, HALF)
            queries = head_lanes(head, q_ref[columns, :]) * SCALE
            scores = contract_cols(k_ref[pl.ds(start, HALF), :], queries.astype(BF))
            finish(scores, vt_ref[lanes, pl.ds(start, HALF)], columns)
        for chunk in range(CONT_TOK // CHUNK):
            first = PROMPT_LENGTH + chunk * CHUNK
            columns = slice(first, first + CHUNK)
            queries = (head_lanes(head, q_ref[columns, :]) * SCALE).astype(BF)
            scores = jnp.concatenate(
                [
                    contract_cols(k_ref[:PROMPT_LENGTH, :], queries),
                    contract_cols(k_ref[PROMPT_LENGTH:, :], queries)
                    + bias_ref[:, chunk * CHUNK : (chunk + 1) * CHUNK],
                ],
                axis=0,
            )
            finish(scores, vt_ref[lanes, :], columns)
    out_ref[...] = ot_ref[...].T.astype(BF)


def backward_kernel(
    flip_ref, qkv_ref, bias_ref, grad_ref, out_ref, lse_ref,
    dqkv_ref, kt_ref, dqt_ref, dka_ref, dva_ref, delta_ref, hooks=(),
):
    q_ref, k_ref, v_ref = thirds(qkv_ref)
    dq_ref, dk_ref, dv_ref = thirds(dqkv_ref)
    kt_ref[...] = k_ref[...].T
    product = (grad_ref[...].astype(F32) * out_ref[...].astype(F32)).T
    for head in range(2):
        lanes = slice(head * HEAD_WIDTH, (head + 1) * HEAD_WIDTH)
        delta_ref[head : head + 1, :] = jnp.sum(product[lanes, :], axis=0, keepdims=True)
    for head in range(2):
        if hooks:
            hooks[head]()
        lanes = slice(head * HEAD_WIDTH, (head + 1) * HEAD_WIDTH)

        def score_grad(scores, values, grads, columns):
            probs = jnp.exp(scores - lse_ref[0, head : head + 1, columns])
            prob_grad = contract_cols(values, grads)
            grad_scores = probs * (prob_grad - delta_ref[head : head + 1, columns])
            return probs.astype(BF), grad_scores.astype(BF)

        for chunk in range(CONT_TOK // CHUNK):
            first = PROMPT_LENGTH + chunk * CHUNK
            columns = slice(first, first + CHUNK)
            queries = (head_lanes(head, q_ref[columns, :]) * SCALE).astype(BF)
            grads = head_lanes(head, grad_ref[columns, :])
            scores = jnp.concatenate(
                [
                    contract_cols(k_ref[:PROMPT_LENGTH, :], queries),
                    contract_cols(k_ref[PROMPT_LENGTH:, :], queries)
                    + bias_ref[:, chunk * CHUNK : (chunk + 1) * CHUNK],
                ],
                axis=0,
            )
            probs, grad_scores = score_grad(scores, v_ref[...], grads, columns)
            dqt_ref[lanes, columns] = matmul(kt_ref[lanes, :], grad_scores) * SCALE
            key_part = matmul(grad_scores, queries)
            value_part = matmul(probs, grads)
            if head == 0 and chunk == 0:
                dka_ref[...] = key_part
                dva_ref[...] = value_part
            else:
                dka_ref[...] += key_part
                dva_ref[...] += value_part
        flip = flip_ref[0, head : head + 1, :] > 0.5
        narrow = flip[:, :LANES]

        def choose(mask, straight, crossed, block):
            return jnp.where(mask, crossed, straight) if block == 0 else jnp.where(mask, straight, crossed)

        key_parts, value_parts = [], []
        for block in range(2):
            columns = slice(block * HALF, (block + 1) * HALF)
            keys = choose(narrow, k_ref[:HALF, :], k_ref[HALF:PROMPT_LENGTH, :], block)
            values = choose(narrow, v_ref[:HALF, :], v_ref[HALF:PROMPT_LENGTH, :], block)
            keys_t = choose(flip, kt_ref[lanes, :HALF], kt_ref[lanes, HALF:PROMPT_LENGTH], block)
            queries = (head_lanes(head, q_ref[columns, :]) * SCALE).astype(BF)
            grads = head_lanes(head, grad_ref[columns, :])
            scores = contract_cols(keys, queries)
            probs, grad_scores = score_grad(scores, values, grads, columns)
            dqt_ref[lanes, columns] = matmul(keys_t, grad_scores) * SCALE
            key_parts.append(matmul(grad_scores, queries))
            value_parts.append(matmul(probs, grads))
        for total_ref, (one, two) in ((dka_ref, key_parts), (dva_ref, value_parts)):
            total_ref[:HALF, :] += choose(narrow, one, two, 0)
            total_ref[HALF:PROMPT_LENGTH, :] += choose(narrow, one, two, 1)
    dq_ref[...] = dqt_ref[...].T.astype(BF)
    dk_ref[...] = dka_ref[...].astype(BF)
    dv_ref[...] = dva_ref[...].astype(BF)


GATHER_CUT = 1152
REDUCE_CUT = 128
BACK_CUT = 1536
VMEM_LIMIT = 56 * 1024 * 1024


def column_spec(lanes):
    return pl.BlockSpec((GROUP_TOK, lanes), lambda i: (0, i))


def flip_spec():
    return pl.BlockSpec((1, 8, HALF), lambda i: (i, 0, 0))


def bias_spec():
    return pl.BlockSpec((CONT_TOK, CONT_TOK), lambda i: (0, 0))


def lse_spec():
    return pl.BlockSpec((1, 8, GROUP_TOK), lambda i: (i, 0, 0))


def attention_forward(perm, qkv, bias):
    width = qkv.shape[1] // 3
    pairs = width // LANES
    return pl.pallas_call(
        forward_kernel,
        grid=(pairs,),
        in_specs=[
            pl.BlockSpec(memory_space=pltpu.SMEM),
            column_spec(3 * LANES),
            bias_spec(),
        ],
        out_specs=[column_spec(LANES), lse_spec()],
        out_shape=[
            jax.ShapeDtypeStruct((GROUP_TOK, width), BF),
            jax.ShapeDtypeStruct((pairs, 8, GROUP_TOK), F32),
        ],
        scratch_shapes=[
            pltpu.VMEM((LANES, GROUP_TOK), BF),
            pltpu.VMEM((LANES, GROUP_TOK), F32),
        ],
        compiler_params=pltpu.CompilerParams(vmem_limit_bytes=VMEM_LIMIT),
        cost_estimate=pl.CostEstimate(
            flops=pairs * 8 * 655360 * 256, bytes_accessed=4 * GROUP_TOK * width * 2, transcendentals=0
        ),
        name="attention_forward",
    )(perm, qkv, bias)


def backward_scratch():
    return [
        pltpu.VMEM((LANES, GROUP_TOK), BF),
        pltpu.VMEM((LANES, GROUP_TOK), F32),
        pltpu.VMEM((GROUP_TOK, LANES), F32),
        pltpu.VMEM((GROUP_TOK, LANES), F32),
        pltpu.VMEM((8, GROUP_TOK), F32),
    ]


def attention_backward(flip, qkv, bias, grads, outs, lse):
    width = qkv.shape[1] // 3
    pairs = width // LANES
    return pl.pallas_call(
        backward_kernel,
        grid=(pairs,),
        in_specs=[
            flip_spec(),
            column_spec(3 * LANES),
            bias_spec(),
            column_spec(LANES),
            column_spec(LANES),
            lse_spec(),
        ],
        out_specs=column_spec(3 * LANES),
        out_shape=jax.ShapeDtypeStruct((GROUP_TOK, 3 * width), BF),
        scratch_shapes=backward_scratch(),
        compiler_params=pltpu.CompilerParams(vmem_limit_bytes=VMEM_LIMIT),
        cost_estimate=pl.CostEstimate(
            flops=pairs * 20 * 655360 * 256, bytes_accessed=8 * GROUP_TOK * width * 2, transcendentals=0
        ),
        name="attention_backward",
    )(flip, qkv, bias, grads, outs, lse)


def gather_kernel(
    size, cut, shard_ref, inputs_ref, own_ref, other_ref, arrived_ref,
    local_sem, swap_sem, z_sem, y_sem, x_sem, near_sem, far_sem, core_sem,
):
    depth = size // 4
    me = lax.axis_index("dp")
    rank = lax.axis_index("tensor")
    z = lax.div(me, 4)
    y = lax.rem(lax.div(me, 2), 2)
    core = lax.rem(me, 2)

    def place(zz, yy, cc):
        return zz * 4 + yy * 2 + cc

    up = {"dp": place(lax.rem(z + 1, depth), y, core)}
    down = {"dp": place(lax.rem(z + depth - 1, depth), y, core)}
    side = {"dp": place(z, 1 - y, core)}
    twin = {"dp": place(z, y, 1 - core)}
    across = {"tensor": 1 - rank}

    barrier = pltpu.get_barrier_semaphore()
    for target in (up, down, side, twin, across):
        pl.semaphore_signal(barrier, inc=1, device_id=target, device_id_type=pl.DeviceIdType.MESH)
    pl.semaphore_wait(barrier, 5)

    started = []

    def send(source, landing, sems, target):
        copy = pltpu.make_async_remote_copy(
            src_ref=source,
            dst_ref=landing,
            send_sem=sems.at[0],
            recv_sem=sems.at[1],
            device_id=target,
            device_id_type=pl.DeviceIdType.MESH,
        )
        copy.start()
        started.append(copy)

    def receive(landing, sems, target):
        pltpu.make_async_remote_copy(
            src_ref=landing,
            dst_ref=landing,
            send_sem=sems.at[0],
            recv_sem=sems.at[1],
            device_id=target,
            device_id_type=pl.DeviceIdType.MESH,
        ).wait_recv()

    keep = pltpu.make_async_copy(shard_ref, own_ref.at[me], local_sem)
    keep.start()

    def slots(age):
        zz = lax.rem(z - age + depth, depth)
        return place(zz, y, core), place(zz, 1 - y, core)

    first = slice(0, cut)
    rest = slice(cut, shard_ref.shape[1])
    for step in range(depth + 2):
        if step < depth:
            mine, _ = slots(step)
            if step == 0:
                block = shard_ref
            else:
                block = own_ref.at[mine]
                receive(block, z_sem.at[step - 1], up)
            if step < depth - 1:
                send(block, own_ref.at[mine], z_sem.at[step], up)
            send(block, own_ref.at[mine], y_sem.at[step], side)
            send(block, other_ref.at[mine], x_sem.at[step], across)
            send(block, own_ref.at[mine], core_sem.at[0, step], twin)
            if step == 0:
                send(inputs_ref.at[1 - rank], arrived_ref, swap_sem, across)
        if 1 <= step <= depth:
            age = step - 1
            mine, beside = slots(age)
            receive(own_ref.at[beside], y_sem.at[age], side)
            send(own_ref.at[beside, :, first], other_ref.at[beside, :, first], near_sem.at[age], across)
            send(own_ref.at[beside], own_ref.at[beside], core_sem.at[1, age], twin)
            receive(other_ref.at[mine], x_sem.at[age], across)
            send(other_ref.at[mine, :, rest], other_ref.at[mine, :, rest], far_sem.at[age], side)
            send(other_ref.at[mine], other_ref.at[mine], core_sem.at[2, age], twin)
        if step >= 2:
            age = step - 2
            _, beside = slots(age)
            receive(other_ref.at[beside, :, first], near_sem.at[age], across)
            receive(other_ref.at[beside, :, rest], far_sem.at[age], side)
            send(other_ref.at[beside], other_ref.at[beside], core_sem.at[3, age], twin)
    receive(arrived_ref, swap_sem, across)
    for age in range(depth):
        zz = lax.rem(z - age + depth, depth)
        here, there = place(zz, y, 1 - core), place(zz, 1 - y, 1 - core)
        receive(own_ref.at[here], core_sem.at[0, age], twin)
        receive(own_ref.at[there], core_sem.at[1, age], twin)
        receive(other_ref.at[here], core_sem.at[2, age], twin)
        receive(other_ref.at[there], core_sem.at[3, age], twin)
    for copy in started:
        copy.wait_send()
    keep.wait()


def gather_weights(shard, inputs, size, cut):
    depth = size // 4
    whole = jax.ShapeDtypeStruct((size,) + shard.shape, shard.dtype)
    sems = pltpu.SemaphoreType.DMA
    return pl.pallas_call(
        functools.partial(gather_kernel, size, cut),
        in_specs=[pl.BlockSpec(memory_space=pl.ANY)] * 2,
        out_specs=[pl.BlockSpec(memory_space=pl.ANY)] * 3,
        out_shape=[whole, whole, jax.ShapeDtypeStruct(inputs.shape[1:], inputs.dtype)],
        scratch_shapes=[
            sems,
            sems((2,)),
            sems((depth - 1, 2)),
            sems((depth, 2)),
            sems((depth, 2)),
            sems((depth, 2)),
            sems((depth, 2)),
            sems((4, depth, 2)),
        ],
        compiler_params=pltpu.CompilerParams(collective_id=0, has_side_effects=True),
        name="gather_weights",
    )(shard, inputs)


class Reducer:
    def __init__(self, size, cut, widths, own, other, totals, scratch):
        (
            self.held, self.got_core, self.got_near, self.got_far, self.got_y, self.got_x, self.got_z,
            self.load_sem, self.core_sem, self.near_sem, self.far_sem, self.y_sem, self.x_sem, self.z_sem,
        ) = scratch
        self.parts = (own, other)
        self.totals = totals
        self.first = slice(0, cut)
        self.rest = slice(cut, sum(widths))
        self.edges = [sum(widths[:i]) for i in range(len(widths) + 1)]
        self.depth = size // 4
        me = lax.axis_index("dp")
        self.z = lax.div(me, 4)
        self.y = lax.rem(lax.div(me, 2), 2)
        self.core = lax.rem(me, 2)
        z, y, core, depth = self.z, self.y, self.core, self.depth
        self.up = {"dp": self.place(lax.rem(z + 1, depth), y, core)}
        self.down = {"dp": self.place(lax.rem(z + depth - 1, depth), y, core)}
        self.side = {"dp": self.place(z, 1 - y, core)}
        self.twin = {"dp": self.place(z, y, 1 - core)}
        self.across = {"tensor": 1 - lax.axis_index("tensor")}

    @staticmethod
    def place(zz, yy, cc):
        return zz * 4 + yy * 2 + cc

    def greet(self):
        barrier = pltpu.get_barrier_semaphore()
        for target in (self.up, self.down, self.side, self.twin, self.across):
            pl.semaphore_signal(barrier, inc=1, device_id=target, device_id_type=pl.DeviceIdType.MESH)
        pl.semaphore_wait(barrier, 5)

    @staticmethod
    def remote(source, landing, sems, target):
        return pltpu.make_async_remote_copy(
            src_ref=source,
            dst_ref=landing,
            send_sem=sems.at[0],
            recv_sem=sems.at[1],
            device_id=target,
            device_id_type=pl.DeviceIdType.MESH,
        )

    def entry(self, slot, age, beside, loads=True):
        zz = lax.rem(self.z + 2 * self.depth - 1 - age, self.depth)
        yy = 1 - self.y if beside else self.y
        copies = []
        for index, source in enumerate(self.parts[slot]):
            columns = slice(self.edges[index], self.edges[index + 1])
            passed = self.remote(
                source.at[self.place(zz, yy, 1 - self.core)],
                self.got_core.at[slot, age, beside, :, columns],
                self.core_sem.at[slot, age, beside, index],
                self.twin,
            )
            load = None
            if loads:
                load = pltpu.make_async_copy(
                    source.at[self.place(zz, yy, self.core)],
                    self.held.at[slot, age, beside, :, columns],
                    self.load_sem.at[slot, age, beside, index],
                )
            copies.append((load, passed))
        return copies

    def near(self, age):
        return self.remote(
            self.held.at[1, age, 1, :, self.first], self.got_near.at[age], self.near_sem.at[age], self.across
        )

    def far(self, age):
        return self.remote(
            self.held.at[1, age, 1, :, self.rest], self.got_far.at[age], self.far_sem.at[age], self.side
        )

    def over_y(self, age):
        return self.remote(self.held.at[0, age, 1], self.got_y.at[age], self.y_sem.at[age], self.side)

    def over_x(self, age):
        return self.remote(self.held.at[1, age, 0], self.got_x.at[age], self.x_sem.at[age], self.across)

    def over_z(self, age):
        return self.remote(self.held.at[0, age, 0], self.got_z.at[age], self.z_sem.at[age], self.up)

    @staticmethod
    def add(target, addend, columns=slice(None)):
        def rows_of(index, carry):
            at = pl.ds(pl.multiple_of(index * 16, 16), 16)
            target[at, columns] = (target[at, columns].astype(F32) + addend[at, :].astype(F32)).astype(BF)
            return carry

        lax.fori_loop(0, target.shape[0] // 16, rows_of, 0)

    def start(self):
        self.greet()
        for age in range(self.depth):
            for beside in (1, 0):
                for slot in (1, 0):
                    for load, passed in self.entry(slot, age, beside):
                        passed.start()
                        load.start()

    def corner(self, age):
        for beside in (1, 0):
            for slot in (1, 0):
                for load, passed in self.entry(slot, age, beside):
                    load.wait()
                    passed.wait_recv()
                self.add(self.held.at[slot, age, beside], self.got_core.at[slot, age, beside])
                if beside and slot:
                    self.near(age).start()
                    self.far(age).start()

    def plane(self, age):
        self.near(age).wait_recv()
        self.add(self.held.at[0, age, 1], self.got_near.at[age], self.first)
        self.over_y(age).start()
        self.far(age).wait_recv()
        self.add(self.held.at[1, age, 0], self.got_far.at[age], self.rest)
        self.over_x(age).start()

    def ring(self, age):
        self.over_y(age).wait_recv()
        self.over_x(age).wait_recv()
        if age:
            self.over_z(age - 1).wait_recv()

        def rows_of(index, carry):
            at = pl.ds(pl.multiple_of(index * 16, 16), 16)
            value = self.held[0, age, 0, at, :].astype(F32) + self.got_y[age, at, :].astype(F32)
            value = value + self.got_x[age, at, :].astype(F32)
            if age:
                value = value + self.got_z[age - 1, at, :].astype(F32)
            if age < self.depth - 1:
                self.held[0, age, 0, at, :] = value.astype(BF)
            else:
                for total, low, high in zip(self.totals, self.edges[:-1], self.edges[1:]):
                    total[at, :] = value[:, low:high]
            return carry

        lax.fori_loop(0, self.held.shape[3] // 16, rows_of, 0)
        if age < self.depth - 1:
            self.over_z(age).start()

    def finish(self):
        for age in range(self.depth):
            for beside in (1, 0):
                for slot in (1, 0):
                    for _, passed in self.entry(slot, age, beside, False):
                        passed.wait_send()
            for copy in (self.near, self.far, self.over_y, self.over_x):
                copy(age).wait_send()
            if age < self.depth - 1:
                self.over_z(age).wait_send()


def reducer_scratch(size, slot, cut, widths):
    depth = size // 4
    wide = sum(widths)
    sems = pltpu.SemaphoreType.DMA
    return [
        pltpu.VMEM((2, depth, 2, slot, wide), BF),
        pltpu.VMEM((2, depth, 2, slot, wide), BF),
        pltpu.VMEM((depth, slot, cut), BF),
        pltpu.VMEM((depth, slot, wide - cut), BF),
        pltpu.VMEM((depth, slot, wide), BF),
        pltpu.VMEM((depth, slot, wide), BF),
        pltpu.VMEM((depth - 1, slot, wide), BF),
        sems((2, depth, 2, len(widths))),
        sems((2, depth, 2, len(widths), 2)),
        sems((depth, 2)),
        sems((depth, 2)),
        sems((depth, 2)),
        sems((depth, 2)),
        sems((depth - 1, 2)),
    ]


def reduce_kernel(size, cut, widths, *refs):
    pieces = len(widths)
    own, other = refs[:pieces], refs[pieces : 2 * pieces]
    rows_ref = refs[2 * pieces]
    totals = refs[2 * pieces + 1 : 3 * pieces + 1]
    arrived_ref, swap_sem = refs[3 * pieces + 1 : 3 * pieces + 3]
    steps = Reducer(size, cut, widths, own, other, totals, refs[3 * pieces + 3 :])
    steps.start()
    swapped = steps.remote(rows_ref, arrived_ref, swap_sem, steps.across)
    swapped.start()
    for step in range(steps.depth + 2):
        if step < steps.depth:
            steps.corner(step)
        if 1 <= step <= steps.depth:
            steps.plane(step - 1)
        if step >= 2:
            steps.ring(step - 2)
    swapped.wait_recv()
    swapped.wait_send()
    steps.finish()


def reduce_blocks(own, other, rows, size, cut):
    slot = own[0].shape[0] // size
    widths = tuple(value.shape[1] for value in own)
    blocks = [value.reshape(size, slot, value.shape[1]) for value in (*own, *other)]
    any_spec = pl.BlockSpec(memory_space=pl.ANY)
    *totals, arrived = pl.pallas_call(
        functools.partial(reduce_kernel, size, cut, widths),
        in_specs=[any_spec] * (len(blocks) + 1),
        out_specs=[pl.BlockSpec(memory_space=pltpu.VMEM)] * len(widths) + [any_spec],
        out_shape=[jax.ShapeDtypeStruct((slot, width), F32) for width in widths]
        + [jax.ShapeDtypeStruct(rows.shape, rows.dtype)],
        scratch_shapes=[pltpu.SemaphoreType.DMA((2,))] + reducer_scratch(size, slot, cut, widths),
        compiler_params=pltpu.CompilerParams(
            collective_id=1, has_side_effects=True, vmem_limit_bytes=VMEM_LIMIT
        ),
        name="reduce_blocks",
    )(*blocks, rows)
    return totals, arrived


PLAN = {
    1: (("corner", 0),),
    2: (("corner", 1), ("corner", 2)),
    3: (("plane", 0), ("corner", 3)),
    4: (("plane", 1),),
    5: (("plane", 2),),
    6: (("plane", 3),),
    7: (("ring", 0),),
    9: (("ring", 1),),
    11: (("ring", 2),),
}


def backward_reduce_kernel(size, cut, widths, flip_ref, bias_ref, *refs):
    own_refs, other_refs = refs[:4], refs[4:8]
    parts = refs[8:12]
    dqkv_ref, outer_ref, inner_ref = refs[12:15]
    work, own_scratch, scratch = refs[15:19], refs[19:24], refs[24:]
    steps = Reducer(size, cut, widths, parts[:2], parts[2:], (outer_ref, inner_ref), scratch)
    at = pl.program_id(0)
    last = pl.num_programs(0) - 1
    pairs = pl.num_programs(0) // 2

    def fill(sources):
        for target, source in zip(work, sources):
            target[...] = source[...]

    @pl.when(at < pairs)
    def _():
        fill(own_refs)

    @pl.when(at >= pairs)
    def _():
        fill(other_refs)

    def hook(head):
        for point, moves in PLAN.items():
            if point % 2 == head:

                @pl.when(at == point // 2)
                def _(moves=moves):
                    for name, age in moves:
                        getattr(steps, name)(age)

    def before():
        @pl.when(at == 0)
        def _():
            steps.start()

        hook(0)

    qkv_ref, grad_ref, out_ref, lse_ref = work
    backward_kernel(
        flip_ref, qkv_ref, bias_ref, grad_ref, out_ref, lse_ref,
        dqkv_ref.at[0], *own_scratch, (before, functools.partial(hook, 1)),
    )

    @pl.when(at == last)
    def _():
        steps.ring(3)
        steps.finish()


def attention_backward_reduce(flips, qkv, bias, grads, outs, lse, own, other, size, cut):
    width = qkv[0].shape[1] // 3
    pairs = width // LANES
    slot = own[0].shape[0] // size
    widths = tuple(value.shape[1] for value in own)
    blocks = [value.reshape(size, slot, value.shape[1]) for value in (*own, *other)]
    any_spec = pl.BlockSpec(memory_space=pl.ANY)

    def half_specs(index):
        return [
            pl.BlockSpec((GROUP_TOK, 3 * LANES), lambda i: (0, index(i))),
            pl.BlockSpec((GROUP_TOK, LANES), lambda i: (0, index(i))),
            pl.BlockSpec((GROUP_TOK, LANES), lambda i: (0, index(i))),
            pl.BlockSpec((1, 8, GROUP_TOK), lambda i: (index(i), 0, 0)),
        ]

    return pl.pallas_call(
        functools.partial(backward_reduce_kernel, size, cut, widths),
        grid=(2 * pairs,),
        in_specs=[
            flip_spec(),
            bias_spec(),
            *half_specs(lambda i: jnp.minimum(i, pairs - 1)),
            *half_specs(lambda i: jnp.maximum(i - pairs, 0)),
            *[any_spec] * 4,
        ],
        out_specs=[
            pl.BlockSpec((1, GROUP_TOK, 3 * LANES), lambda i: (i // pairs, 0, i % pairs)),
            *[pl.BlockSpec((slot, value), lambda i: (0, 0)) for value in widths],
        ],
        out_shape=[
            jax.ShapeDtypeStruct((2, GROUP_TOK, 3 * width), BF),
            *[jax.ShapeDtypeStruct((slot, value), F32) for value in widths],
        ],
        scratch_shapes=[
            pltpu.VMEM((GROUP_TOK, 3 * LANES), BF),
            pltpu.VMEM((GROUP_TOK, LANES), BF),
            pltpu.VMEM((GROUP_TOK, LANES), BF),
            pltpu.VMEM((1, 8, GROUP_TOK), F32),
        ]
        + backward_scratch()
        + reducer_scratch(size, slot, cut, widths),
        compiler_params=pltpu.CompilerParams(
            collective_id=2, has_side_effects=True, vmem_limit_bytes=VMEM_LIMIT
        ),
        name="attention_backward_reduce",
    )(
        jnp.concatenate(flips),
        bias,
        qkv[0], grads[0], outs[0], lse[0],
        qkv[1], grads[1], outs[1], lse[1],
        *blocks,
    )


def swap_pair(value):
    return lax.ppermute(value, "tensor", [(0, 1), (1, 0)])


def swap_bit(value, bit, size):
    return lax.ppermute(value, "dp", [(i, i ^ (1 << bit)) for i in range(size)])


def pick(stacked, index, axis=0):
    return lax.dynamic_index_in_dim(stacked, index, axis, keepdims=False)


def reduce_tree(own, other, order, size, last_type=F32):
    bits = size.bit_length() - 1
    me = lax.axis_index("dp")
    held = [value.reshape((2,) * bits + (value.shape[0] // size,) + value.shape[1:]) for value in (own, other)]
    left = list(range(bits - 1, -1, -1))
    for step, move in enumerate(order):
        kind = last_type if step == len(order) - 1 else own.dtype
        if move == "t":
            arrived = swap_pair(held[1])
            held = [(held[0].astype(F32) + arrived.astype(F32)).astype(kind)]
            continue
        axis = left.index(move)
        left.remove(move)
        mine = lax.rem(lax.div(me, 1 << move), 2)
        arrived = [swap_bit(pick(value, 1 - mine, axis), move, size) for value in held]
        held = [
            (pick(value, mine, axis).astype(F32) + got.astype(F32)).astype(kind)
            for value, got in zip(held, arrived)
        ]
    return held[0]


def tree_order(size, pair_first):
    bits = size.bit_length() - 1
    rest = list(range(bits - 1, 1, -1))
    if pair_first:
        return [0, "t", 1] + rest
    return [0, 1, "t"] + rest


def local(
    inputs,
    cotangent,
    seg_ids,
    block_perm,
    query_weight,
    key_weight,
    value_weight,
    output_weight,
    inner_weight,
    outer_weight,
    first_gain,
    first_shift,
    second_gain,
    second_shift,
    size,
):
    rank = lax.axis_index("tensor")
    at_first = rank == 0

    def both(stacked):
        return pick(stacked, rank), pick(stacked, 1 - rank)

    width = query_weight.shape[1]
    hidden_width = inner_weight.shape[1]
    slot = query_weight.shape[0]
    vectors = jnp.concatenate([first_gain, first_shift, second_gain, second_shift])
    per_vector = first_gain.shape[0]
    order = block_perm.reshape(-1).astype(BF)
    vector_block = jnp.concatenate(
        [jnp.pad(value[None, :], ((0, 0), (0, 128 - value.shape[0]))) for value in (vectors, order)]
        + [jnp.zeros((slot - 2, 128), BF)]
    )
    by_pair = jnp.stack(
        [value.reshape(slot, -1, LANES) for value in (query_weight, key_weight, value_weight)], axis=2
    ).reshape(slot, 3 * width)
    shard = jnp.concatenate(
        [by_pair, output_weight.T, vector_block, inner_weight, outer_weight.T], axis=1
    )
    own, other, arrived_rows = gather_weights(shard, inputs, size, GATHER_CUT)
    flat = [value.reshape(-1, value.shape[-1]) for value in (own, other)]
    edges = [0, 3 * width, 4 * width, 4 * width + 128, 4 * width + 128 + hidden_width, shard.shape[1]]
    w_qkv, w_output, vector_rows, w_inner, w_outer = [
        [value[:, low:high] for value in flat] for low, high in zip(edges[:-1], edges[1:])
    ]
    perms = [value[1, : order.shape[0]].astype(jnp.int32).reshape(block_perm.shape) for value in vector_rows]
    vector_rows = [value.reshape(size, slot, 128)[:, 0, : 4 * per_vector] for value in vector_rows]
    all_vectors = jnp.stack(
        [jnp.where(at_first, *vector_rows), jnp.where(at_first, *vector_rows[::-1])], axis=1
    )
    all_vectors = all_vectors.reshape(size, 2, 4, per_vector).transpose(2, 0, 1, 3).reshape(4, -1)
    gain_one, shift_one, gain_two, shift_two = [all_vectors[i].astype(F32) for i in range(4)]

    def collect(mine_and_other, arrived):
        mine = pick(mine_and_other, rank)
        return jnp.concatenate(
            [jnp.where(at_first, mine, arrived), jnp.where(at_first, arrived, mine)], axis=0
        )

    def spread(rows, arrived=None):
        halves = rows.reshape((2, rows.shape[0] // 2) + rows.shape[1:])
        mine = pick(halves, rank)
        if arrived is None:
            arrived = swap_pair(pick(halves, 1 - rank).astype(BF))
        arrived = arrived.astype(rows.dtype)
        return jnp.stack([jnp.where(at_first, mine, arrived), jnp.where(at_first, arrived, mine)])

    rows = collect(inputs, arrived_rows)
    segments = pick(seg_ids, rank)[0]
    bias = jnp.where(segments[:, None] == segments[None, :], 0.0, MASKED).astype(F32)

    qkv = [matmul(rows, weight).astype(BF) for weight in w_qkv]
    qkv[0], late = lax.optimization_barrier((qkv[0], pick(cotangent, 1 - rank)))
    late = swap_pair(late)
    attended, lse = zip(*[attention_forward(p, value, bias) for p, value in zip(perms, qkv)])
    attention_sum = contract_cols(attended[0], w_output[0]) + contract_cols(attended[1], w_output[1])
    attention_sum, late = lax.optimization_barrier((attention_sum, late))
    upstream = collect(cotangent, late).astype(F32)
    hidden, unit_one, inverse_one = normalize(rows.astype(F32) + attention_sum, gain_one, shift_one)
    hidden_low = hidden.astype(BF)
    activated, slope = zip(*[gelu_pair(matmul(hidden_low, weight)) for weight in w_inner])
    activated = [value.astype(BF) for value in activated]
    slope = [value.astype(BF) for value in slope]
    branch = contract_cols(activated[0], w_outer[0]) + contract_cols(activated[1], w_outer[1])
    layer_out, unit_two, inverse_two = normalize(hidden + branch, gain_two, shift_two)
    layer_low = layer_out.astype(BF)
    layer_leaving = pick(layer_low.reshape(4, -1, layer_low.shape[1]).reshape(2, 2, -1, layer_low.shape[1]), 1 - rank)
    layer_first = swap_pair(layer_leaving[0])

    second_back = normalize_back(upstream, unit_two, inverse_two, gain_two)
    branch_grad = second_back.astype(BF)
    outer_terms = [contract_rows(branch_grad, value).astype(BF) for value in activated]
    pre_grad = [
        (matmul(branch_grad, weight) * part.astype(F32)).astype(BF) for weight, part in zip(w_outer, slope)
    ]
    layer_first, pre_grad[1] = lax.optimization_barrier((layer_first, pre_grad[1]))
    layer_second, layer_first = lax.optimization_barrier((layer_leaving[1], layer_first))
    layer_second = swap_pair(layer_second)
    inner_terms = [contract_rows(hidden_low, value).astype(BF) for value in pre_grad]
    hidden_back = second_back + contract_cols(pre_grad[0], w_inner[0]) + contract_cols(pre_grad[1], w_inner[1])
    first_back = normalize_back(hidden_back, unit_one, inverse_one, gain_one)
    norm_terms = jnp.stack(
        [
            jnp.sum(hidden_back * unit_one, axis=0),
            jnp.sum(hidden_back, axis=0),
            jnp.sum(upstream * unit_two, axis=0),
            jnp.sum(upstream, axis=0),
        ]
    )
    by_shard = norm_terms.reshape(4, size, 2, per_vector).transpose(2, 1, 0, 3).reshape(2, size, 4, per_vector)
    vector_terms = [
        jnp.pad(value.reshape(size, 1, 4 * per_vector), ((0, 0), (0, slot - 1), (0, 128 - 4 * per_vector)))
        .reshape(size * slot, 128)
        .astype(BF)
        for value in both(by_shard)
    ]

    attention_grad = first_back.astype(BF)
    output_terms = [contract_rows(attention_grad, value).astype(BF) for value in attended]
    attended_grad = [matmul(attention_grad, weight).astype(BF) for weight in w_output]
    layer_second, attended_grad[0] = lax.optimization_barrier((layer_second, attended_grad[0]))
    layer_arrived = jnp.concatenate([layer_first, layer_second])
    layer_rows = spread(layer_low, layer_arrived)
    flips = [
        jnp.broadcast_to(
            jnp.pad(value[:, 0].astype(F32).reshape(-1, 2), ((0, 0), (0, 6)))[:, :, None],
            (value.shape[0] // 2, 8, HALF),
        )
        for value in perms
    ]
    fast = size == 16 and slot % 16 == 0
    if fast:
        head_grads, grad_outer, grad_inner = attention_backward_reduce(
            flips, qkv, bias, attended_grad, attended, lse, *zip(outer_terms, inner_terms), size, BACK_CUT
        )
    else:
        operands = zip(flips, qkv, [bias] * 2, attended_grad, attended, lse)
        head_grads = [attention_backward(*values) for values in operands]
    head_terms = [contract_rows(rows, value).astype(BF) for value in head_grads]
    input_grad = first_back + contract_cols(head_grads[0], w_qkv[0]) + contract_cols(head_grads[1], w_qkv[1])
    def put(rows_out, value, index):
        return lax.dynamic_update_slice(rows_out, value[None], (index, 0, 0))

    halves = input_grad.reshape(2, GROUP_TOK // 2, -1)
    leaving = pick(halves, 1 - rank).astype(BF)
    terms = list(zip(output_terms, vector_terms, head_terms))
    if fast:
        (grad_output, norm_rows, grad_heads), arrived = reduce_blocks(*terms, leaving, size, REDUCE_CUT)
    else:
        terms = [(outer, inner, *rest) for outer, inner, rest in zip(outer_terms, inner_terms, terms)]
        packed = [jnp.concatenate(value, axis=1) for value in terms]
        total, arrived = reduce_tree(*packed, tree_order(size, True), size), swap_pair(leaving)
        total = total.reshape(slot, -1)
        edges = [0]
        for value in terms[0]:
            edges.append(edges[-1] + value.shape[1])
        grad_outer, grad_inner, grad_output, norm_rows, grad_heads = [
            total[:, low:high] for low, high in zip(edges[:-1], edges[1:])
        ]
    input_rows = put(put(jnp.zeros_like(halves), pick(halves, rank), rank), arrived.astype(F32), 1 - rank)
    grad_heads = grad_heads.reshape(slot, -1, 3, LANES)
    grad_query, grad_key, grad_value = [grad_heads[:, :, i].reshape(slot, width) for i in range(3)]
    norm_shards = norm_rows[0, : 4 * per_vector].reshape(4, per_vector)
    return (
        layer_rows,
        input_rows,
        grad_query,
        grad_key,
        grad_value,
        grad_output.T,
        grad_inner,
        grad_outer.T,
        norm_shards[0],
        norm_shards[1],
        norm_shards[2],
        norm_shards[3],
    )


def solution(mesh):
    rows = P(None, ("dp", "tensor"), None)
    columns = P("dp", "tensor")
    flipped = P("tensor", "dp")
    vector = P(("dp", "tensor"))
    return jax.shard_map(
        functools.partial(local, size=mesh.shape["dp"]),
        mesh=mesh,
        in_specs=(
            rows, rows, P(None, "dp", None), P("tensor", None),
            columns, columns, columns, flipped, columns, flipped,
            vector, vector, vector, vector,
        ),
        out_specs=(
            rows, rows, columns, columns, columns, flipped, columns, flipped,
            vector, vector, vector, vector,
        ),
        check_vma=False,
    )
```

```python
import functools
import math

import jax
import jax.numpy as jnp
from jax import lax
from jax.experimental import pallas as pl
from jax.experimental.pallas import tpu as pltpu
from jax.sharding import PartitionSpec as P

HEAD_WIDTH = 64
PROMPT_LENGTH = 512
CONT_TOK = 512
GROUP_TOK = PROMPT_LENGTH + CONT_TOK
HALF = PROMPT_LENGTH // 2
LANES = 2 * HEAD_WIDTH
CHUNK = 256

EPSILON = 1e-05
MASKED = -1e30
SCALE = 1.0 / math.sqrt(HEAD_WIDTH)
ROOT_HALF = 1.0 / math.sqrt(2.0)
ROOT_TWO_PI = 1.0 / math.sqrt(2.0 * math.pi)


BF = jnp.bfloat16
F32 = jnp.float32


def dot(left, right, dims):
    return lax.dot_general(left, right, (dims, ((), ())), preferred_element_type=F32)


def matmul(left, right):
    return dot(left, right, ((1,), (0,)))


def contract_rows(left, right):
    return dot(left, right, ((0,), (0,)))


def contract_cols(left, right):
    return dot(left, right, ((1,), (1,)))


def normalize(residual, gain_vector, shift_vector):
    centred = residual - jnp.mean(residual, axis=-1, keepdims=True)
    inverse = lax.rsqrt(jnp.mean(centred * centred, axis=-1, keepdims=True) + EPSILON)
    unit_rows = centred * inverse
    return (unit_rows * gain_vector + shift_vector, unit_rows, inverse)


def normalize_back(upstream, unit_rows, inverse, gain_vector):
    scaled = upstream * gain_vector
    first_mean = jnp.mean(scaled, axis=-1, keepdims=True)
    second_mean = jnp.mean(scaled * unit_rows, axis=-1, keepdims=True)
    return inverse * (scaled - first_mean - unit_rows * second_mean)


def gelu_pair(values):
    normal_cdf = 0.5 * (1.0 + lax.erf(values * ROOT_HALF))
    density = jnp.exp(-0.5 * values * values) * ROOT_TWO_PI
    return (values * normal_cdf, normal_cdf + values * density)


def head_lanes(head, value):
    lane = lax.broadcasted_iota(jnp.int32, value.shape, 1)
    return jnp.where((lane // HEAD_WIDTH) == head, value, jnp.zeros_like(value))


def thirds(ref):
    return [ref.at[:, i * LANES : (i + 1) * LANES] for i in range(3)]


def forward_kernel(perm_ref, qkv_ref, bias_ref, out_ref, lse_ref, vt_ref, ot_ref):
    pair = pl.program_id(0)
    q_ref, k_ref, v_ref = thirds(qkv_ref)
    vt_ref[...] = v_ref[...].T
    for head in range(2):
        lanes = slice(head * HEAD_WIDTH, (head + 1) * HEAD_WIDTH)

        def finish(scores, values_t, columns):
            top = jnp.max(scores, axis=0, keepdims=True)
            weights = jnp.exp(scores - top)
            total = jnp.sum(weights, axis=0, keepdims=True)
            out_t = matmul(values_t, weights.astype(BF))
            ot_ref[lanes, columns] = out_t / total
            lse_ref[0, head : head + 1, columns] = top + jnp.log(total)

        for block in range(2):
            columns = slice(block * HALF, (block + 1) * HALF)
            start = pl.multiple_of(perm_ref[pair * 2 + head, block] * HALF, HALF)
            queries = head_lanes(head, q_ref[columns, :]) * SCALE
            scores = contract_cols(k_ref[pl.ds(start, HALF), :], queries.astype(BF))
            finish(scores, vt_ref[lanes, pl.ds(start, HALF)], columns)
        for chunk in range(CONT_TOK // CHUNK):
            first = PROMPT_LENGTH + chunk * CHUNK
            columns = slice(first, first + CHUNK)
            queries = (head_lanes(head, q_ref[columns, :]) * SCALE).astype(BF)
            scores = jnp.concatenate(
                [
                    contract_cols(k_ref[:PROMPT_LENGTH, :], queries),
                    contract_cols(k_ref[PROMPT_LENGTH:, :], queries)
                    + bias_ref[:, chunk * CHUNK : (chunk + 1) * CHUNK],
                ],
                axis=0,
            )
            finish(scores, vt_ref[lanes, :], columns)
    out_ref[...] = ot_ref[...].T.astype(BF)


def backward_kernel(
    flip_ref, qkv_ref, bias_ref, grad_ref, out_ref, lse_ref,
    dqkv_ref, kt_ref, dqt_ref, dka_ref, dva_ref, delta_ref, hooks=(),
):
    q_ref, k_ref, v_ref = thirds(qkv_ref)
    dq_ref, dk_ref, dv_ref = thirds(dqkv_ref)
    kt_ref[...] = k_ref[...].T
    product = (grad_ref[...].astype(F32) * out_ref[...].astype(F32)).T
    for head in range(2):
        lanes = slice(head * HEAD_WIDTH, (head + 1) * HEAD_WIDTH)
        delta_ref[head : head + 1, :] = jnp.sum(product[lanes, :], axis=0, keepdims=True)
    for head in range(2):
        if hooks:
            hooks[head]()
        lanes = slice(head * HEAD_WIDTH, (head + 1) * HEAD_WIDTH)

        def score_grad(scores, values, grads, columns):
            probs = jnp.exp(scores - lse_ref[0, head : head + 1, columns])
            prob_grad = contract_cols(values, grads)
            grad_scores = probs * (prob_grad - delta_ref[head : head + 1, columns])
            return probs.astype(BF), grad_scores.astype(BF)

        for chunk in range(CONT_TOK // CHUNK):
            first = PROMPT_LENGTH + chunk * CHUNK
            columns = slice(first, first + CHUNK)
            queries = (head_lanes(head, q_ref[columns, :]) * SCALE).astype(BF)
            grads = head_lanes(head, grad_ref[columns, :])
            scores = jnp.concatenate(
                [
                    contract_cols(k_ref[:PROMPT_LENGTH, :], queries),
                    contract_cols(k_ref[PROMPT_LENGTH:, :], queries)
                    + bias_ref[:, chunk * CHUNK : (chunk + 1) * CHUNK],
                ],
                axis=0,
            )
            probs, grad_scores = score_grad(scores, v_ref[...], grads, columns)
            dqt_ref[lanes, columns] = matmul(kt_ref[lanes, :], grad_scores) * SCALE
            key_part = matmul(grad_scores, queries)
            value_part = matmul(probs, grads)
            if head == 0 and chunk == 0:
                dka_ref[...] = key_part
                dva_ref[...] = value_part
            else:
                dka_ref[...] += key_part
                dva_ref[...] += value_part
        flip = flip_ref[0, head : head + 1, :] > 0.5
        narrow = flip[:, :LANES]

        def choose(mask, straight, crossed, block):
            return jnp.where(mask, crossed, straight) if block == 0 else jnp.where(mask, straight, crossed)

        key_parts, value_parts = [], []
        for block in range(2):
            columns = slice(block * HALF, (block + 1) * HALF)
            keys = choose(narrow, k_ref[:HALF, :], k_ref[HALF:PROMPT_LENGTH, :], block)
            values = choose(narrow, v_ref[:HALF, :], v_ref[HALF:PROMPT_LENGTH, :], block)
            keys_t = choose(flip, kt_ref[lanes, :HALF], kt_ref[lanes, HALF:PROMPT_LENGTH], block)
            queries = (head_lanes(head, q_ref[columns, :]) * SCALE).astype(BF)
            grads = head_lanes(head, grad_ref[columns, :])
            scores = contract_cols(keys, queries)
            probs, grad_scores = score_grad(scores, values, grads, columns)
            dqt_ref[lanes, columns] = matmul(keys_t, grad_scores) * SCALE
            key_parts.append(matmul(grad_scores, queries))
            value_parts.append(matmul(probs, grads))
        for total_ref, (one, two) in ((dka_ref, key_parts), (dva_ref, value_parts)):
            total_ref[:HALF, :] += choose(narrow, one, two, 0)
            total_ref[HALF:PROMPT_LENGTH, :] += choose(narrow, one, two, 1)
    dq_ref[...] = dqt_ref[...].T.astype(BF)
    dk_ref[...] = dka_ref[...].astype(BF)
    dv_ref[...] = dva_ref[...].astype(BF)


GATHER_CUT = 640
LATE = 1408
LATE_CUT = 640
REDUCE_CUT = 128
BACK_CUT = 1536
VMEM_LIMIT = 56 * 1024 * 1024


def column_spec(lanes):
    return pl.BlockSpec((GROUP_TOK, lanes), lambda i: (0, i))


def flip_spec():
    return pl.BlockSpec((1, 8, HALF), lambda i: (i, 0, 0))


def bias_spec():
    return pl.BlockSpec((CONT_TOK, CONT_TOK), lambda i: (0, 0))


def lse_spec():
    return pl.BlockSpec((1, 8, GROUP_TOK), lambda i: (i, 0, 0))


def attention_forward(perm, qkv, bias):
    width = qkv.shape[1] // 3
    pairs = width // LANES
    return pl.pallas_call(
        forward_kernel,
        grid=(pairs,),
        in_specs=[
            pl.BlockSpec(memory_space=pltpu.SMEM),
            column_spec(3 * LANES),
            bias_spec(),
        ],
        out_specs=[column_spec(LANES), lse_spec()],
        out_shape=[
            jax.ShapeDtypeStruct((GROUP_TOK, width), BF),
            jax.ShapeDtypeStruct((pairs, 8, GROUP_TOK), F32),
        ],
        scratch_shapes=[
            pltpu.VMEM((LANES, GROUP_TOK), BF),
            pltpu.VMEM((LANES, GROUP_TOK), F32),
        ],
        compiler_params=pltpu.CompilerParams(vmem_limit_bytes=VMEM_LIMIT),
        cost_estimate=pl.CostEstimate(
            flops=pairs * 8 * 655360 * 256, bytes_accessed=4 * GROUP_TOK * width * 2, transcendentals=0
        ),
        name="attention_forward",
    )(perm, qkv, bias)


def backward_scratch():
    return [
        pltpu.VMEM((LANES, GROUP_TOK), BF),
        pltpu.VMEM((LANES, GROUP_TOK), F32),
        pltpu.VMEM((GROUP_TOK, LANES), F32),
        pltpu.VMEM((GROUP_TOK, LANES), F32),
        pltpu.VMEM((8, GROUP_TOK), F32),
    ]


def attention_backward(flip, qkv, bias, grads, outs, lse):
    width = qkv.shape[1] // 3
    pairs = width // LANES
    return pl.pallas_call(
        backward_kernel,
        grid=(pairs,),
        in_specs=[
            flip_spec(),
            column_spec(3 * LANES),
            bias_spec(),
            column_spec(LANES),
            column_spec(LANES),
            lse_spec(),
        ],
        out_specs=column_spec(3 * LANES),
        out_shape=jax.ShapeDtypeStruct((GROUP_TOK, 3 * width), BF),
        scratch_shapes=backward_scratch(),
        compiler_params=pltpu.CompilerParams(vmem_limit_bytes=VMEM_LIMIT),
        cost_estimate=pl.CostEstimate(
            flops=pairs * 20 * 655360 * 256, bytes_accessed=8 * GROUP_TOK * width * 2, transcendentals=0
        ),
        name="attention_backward",
    )(flip, qkv, bias, grads, outs, lse)


def gather_kernel(
    size, plan, places, *refs,
):
    pieces = refs[: len(plan)]
    inputs_ref, own_ref, other_ref, arrived_ref, shard_ref = refs[len(plan) : len(plan) + 5]
    (
        load_sem, local_sem, swap_sem, z_sem, y_sem, x_sem, near_sem, far_sem, core_sem,
        late_z, late_y, late_x, late_near, late_far, late_core,
    ) = refs[len(plan) + 5 :]
    cut, base, late_cut, wide = places
    loads = []
    for piece, moves in zip(pieces, plan):
        for source, landing, width in moves:
            load = pltpu.make_async_copy(
                piece.at[:, source : source + width],
                shard_ref.at[:, landing : landing + width],
                load_sem.at[len(loads)],
            )
            load.start()
            loads.append(load)
    depth = size // 4
    me = lax.axis_index("dp")
    rank = lax.axis_index("tensor")
    z = lax.div(me, 4)
    y = lax.rem(lax.div(me, 2), 2)
    core = lax.rem(me, 2)

    def place(zz, yy, cc):
        return zz * 4 + yy * 2 + cc

    up = {"dp": place(lax.rem(z + 1, depth), y, core)}
    down = {"dp": place(lax.rem(z + depth - 1, depth), y, core)}
    side = {"dp": place(z, 1 - y, core)}
    twin = {"dp": place(z, y, 1 - core)}
    across = {"tensor": 1 - rank}

    barrier = pltpu.get_barrier_semaphore()
    for target in (up, down, side, twin, across):
        pl.semaphore_signal(barrier, inc=1, device_id=target, device_id_type=pl.DeviceIdType.MESH)
    pl.semaphore_wait(barrier, 5)

    started = []

    def send(source, landing, sems, target):
        copy = pltpu.make_async_remote_copy(
            src_ref=source,
            dst_ref=landing,
            send_sem=sems.at[0],
            recv_sem=sems.at[1],
            device_id=target,
            device_id_type=pl.DeviceIdType.MESH,
        )
        copy.start()
        started.append(copy)

    def receive(landing, sems, target):
        pltpu.make_async_remote_copy(
            src_ref=landing,
            dst_ref=landing,
            send_sem=sems.at[0],
            recv_sem=sems.at[1],
            device_id=target,
            device_id_type=pl.DeviceIdType.MESH,
        ).wait_recv()

    for load in loads:
        load.wait()
    keep = pltpu.make_async_copy(shard_ref, own_ref.at[me], local_sem)
    keep.start()

    def slots(age):
        zz = lax.rem(z - age + depth, depth)
        return place(zz, y, core), place(zz, 1 - y, core)

    early = slice(0, base)
    late = slice(base, wide)
    first, rest = slice(0, cut), slice(cut, base)
    late_first, late_rest = slice(base, late_cut), slice(late_cut, wide)

    def late_block(kind, age, columns=late):
        half = own_ref if kind < 2 else other_ref
        return half.at[slots(age)[kind % 2], :, columns]

    def pass_late(kind, age, block=None):
        landing = late_block(kind, age)
        block = landing if block is None else block
        if age < depth - 1:
            send(block, landing, late_z.at[kind, age], up)
        send(block, landing, late_core.at[kind, age], twin)

    for step in range(depth + 2):
        if step < depth:
            mine, _ = slots(step)
            landing = own_ref.at[mine, :, early]
            if step == 0:
                block = shard_ref.at[:, early]
            else:
                block = landing
                receive(block, z_sem.at[step - 1], up)
            if step < depth - 1:
                send(block, landing, z_sem.at[step], up)
            if step == 0:
                send(shard_ref.at[:, late], late_block(0, 0), late_y, side)
                send(shard_ref.at[:, late], late_block(2, 0), late_x, across)
                pass_late(0, 0, shard_ref.at[:, late])
            send(block, landing, y_sem.at[step], side)
            send(block, other_ref.at[mine, :, early], x_sem.at[step], across)
            send(block, landing, core_sem.at[0, step], twin)
            if step == 0:
                send(inputs_ref.at[1 - rank], arrived_ref, swap_sem, across)
        if step == 1:
            receive(late_block(1, 0), late_y, side)
            send(late_block(1, 0, late_first), late_block(3, 0, late_first), late_near, across)
            pass_late(1, 0)
            receive(late_block(2, 0), late_x, across)
            mine, _ = slots(0)
            send(other_ref.at[mine, :, late_rest], other_ref.at[mine, :, late_rest], late_far, side)
            pass_late(2, 0)
        if 2 <= step <= depth:
            for kind in range(3):
                receive(late_block(kind, step - 1), late_z.at[kind, step - 2], up)
                pass_late(kind, step - 1)
        if step >= 2:
            if step == 2:
                receive(late_block(3, 0, late_first), late_near, across)
                receive(late_block(3, 0, late_rest), late_far, side)
            else:
                receive(late_block(3, step - 2), late_z.at[3, step - 3], up)
            pass_late(3, step - 2)
        if 1 <= step <= depth:
            age = step - 1
            mine, beside = slots(age)
            block = own_ref.at[beside, :, early]
            receive(block, y_sem.at[age], side)
            send(own_ref.at[beside, :, first], other_ref.at[beside, :, first], near_sem.at[age], across)
            send(block, block, core_sem.at[1, age], twin)
            block = other_ref.at[mine, :, early]
            receive(block, x_sem.at[age], across)
            send(other_ref.at[mine, :, rest], other_ref.at[mine, :, rest], far_sem.at[age], side)
            send(block, block, core_sem.at[2, age], twin)
        if step >= 2:
            age = step - 2
            _, beside = slots(age)
            receive(other_ref.at[beside, :, first], near_sem.at[age], across)
            receive(other_ref.at[beside, :, rest], far_sem.at[age], side)
            block = other_ref.at[beside, :, early]
            send(block, block, core_sem.at[3, age], twin)
    receive(arrived_ref, swap_sem, across)
    for age in range(depth):
        zz = lax.rem(z - age + depth, depth)
        here, there = place(zz, y, 1 - core), place(zz, 1 - y, 1 - core)
        blocks = (own_ref.at[here], own_ref.at[there], other_ref.at[here], other_ref.at[there])
        for kind, block in enumerate(blocks):
            receive(block.at[:, early], core_sem.at[kind, age], twin)
            receive(block.at[:, late], late_core.at[kind, age], twin)
    for copy in started:
        copy.wait_send()
    keep.wait()


def gather_weights(pieces, plan, inputs, size):
    depth = size // 4
    slot = pieces[0].shape[0]
    moves = [move for piece in plan for move in piece]
    wide = sum(width for _, _, width in moves)
    whole = jax.ShapeDtypeStruct((size, slot, wide), BF)
    sems = pltpu.SemaphoreType.DMA
    base = wide - LATE
    return pl.pallas_call(
        functools.partial(gather_kernel, size, plan, (GATHER_CUT, base, base + LATE_CUT, wide)),
        in_specs=[pl.BlockSpec(memory_space=pl.ANY)] * (len(pieces) + 1),
        out_specs=[pl.BlockSpec(memory_space=pl.ANY)] * 3,
        out_shape=[whole, whole, jax.ShapeDtypeStruct(inputs.shape[1:], inputs.dtype)],
        scratch_shapes=[
            pltpu.VMEM((slot, wide), BF),
            sems((len(moves),)),
            sems,
            sems((2,)),
            sems((depth - 1, 2)),
            sems((depth, 2)),
            sems((depth, 2)),
            sems((depth, 2)),
            sems((depth, 2)),
            sems((4, depth, 2)),
            sems((4, depth - 1, 2)),
            sems((2,)),
            sems((2,)),
            sems((2,)),
            sems((2,)),
            sems((4, depth, 2)),
        ],
        compiler_params=pltpu.CompilerParams(collective_id=0, has_side_effects=True),
        name="gather_weights",
    )(*pieces, inputs)


class Reducer:
    def __init__(self, size, cut, widths, own, other, totals, scratch):
        (
            self.held, self.got_core, self.got_near, self.got_far, self.got_y, self.got_x, self.got_z,
            self.load_sem, self.core_sem, self.near_sem, self.far_sem, self.y_sem, self.x_sem, self.z_sem,
        ) = scratch
        self.parts = (own, other)
        self.totals = totals
        self.first = slice(0, cut)
        self.rest = slice(cut, sum(widths))
        self.edges = [sum(widths[:i]) for i in range(len(widths) + 1)]
        self.depth = size // 4
        me = lax.axis_index("dp")
        self.z = lax.div(me, 4)
        self.y = lax.rem(lax.div(me, 2), 2)
        self.core = lax.rem(me, 2)
        z, y, core, depth = self.z, self.y, self.core, self.depth
        self.up = {"dp": self.place(lax.rem(z + 1, depth), y, core)}
        self.down = {"dp": self.place(lax.rem(z + depth - 1, depth), y, core)}
        self.side = {"dp": self.place(z, 1 - y, core)}
        self.twin = {"dp": self.place(z, y, 1 - core)}
        self.across = {"tensor": 1 - lax.axis_index("tensor")}

    @staticmethod
    def place(zz, yy, cc):
        return zz * 4 + yy * 2 + cc

    def greet(self):
        barrier = pltpu.get_barrier_semaphore()
        for target in (self.up, self.down, self.side, self.twin, self.across):
            pl.semaphore_signal(barrier, inc=1, device_id=target, device_id_type=pl.DeviceIdType.MESH)
        pl.semaphore_wait(barrier, 5)

    @staticmethod
    def remote(source, landing, sems, target):
        return pltpu.make_async_remote_copy(
            src_ref=source,
            dst_ref=landing,
            send_sem=sems.at[0],
            recv_sem=sems.at[1],
            device_id=target,
            device_id_type=pl.DeviceIdType.MESH,
        )

    def entry(self, slot, age, beside, loads=True):
        zz = lax.rem(self.z + 2 * self.depth - 1 - age, self.depth)
        yy = 1 - self.y if beside else self.y
        copies = []
        for index, source in enumerate(self.parts[slot]):
            columns = slice(self.edges[index], self.edges[index + 1])
            passed = self.remote(
                source.at[self.place(zz, yy, 1 - self.core)],
                self.got_core.at[slot, age, beside, :, columns],
                self.core_sem.at[slot, age, beside, index],
                self.twin,
            )
            load = None
            if loads:
                load = pltpu.make_async_copy(
                    source.at[self.place(zz, yy, self.core)],
                    self.held.at[slot, age, beside, :, columns],
                    self.load_sem.at[slot, age, beside, index],
                )
            copies.append((load, passed))
        return copies

    def near(self, age):
        return self.remote(
            self.held.at[1, age, 1, :, self.first], self.got_near.at[age], self.near_sem.at[age], self.across
        )

    def far(self, age):
        return self.remote(
            self.held.at[1, age, 1, :, self.rest], self.got_far.at[age], self.far_sem.at[age], self.side
        )

    def over_y(self, age):
        return self.remote(self.held.at[0, age, 1], self.got_y.at[age], self.y_sem.at[age], self.side)

    def over_x(self, age):
        return self.remote(self.held.at[1, age, 0], self.got_x.at[age], self.x_sem.at[age], self.across)

    def over_z(self, age):
        return self.remote(self.held.at[0, age, 0], self.got_z.at[age], self.z_sem.at[age], self.up)

    @staticmethod
    def add(target, addend, columns=slice(None)):
        def rows_of(index, carry):
            at = pl.ds(pl.multiple_of(index * 16, 16), 16)
            target[at, columns] = (target[at, columns].astype(F32) + addend[at, :].astype(F32)).astype(BF)
            return carry

        lax.fori_loop(0, target.shape[0] // 16, rows_of, 0)

    def start(self):
        self.greet()
        for age in range(self.depth):
            for beside in (1, 0):
                for slot in (1, 0):
                    for load, passed in self.entry(slot, age, beside):
                        passed.start()
                        load.start()

    def corner(self, age):
        for beside in (1, 0):
            for slot in (1, 0):
                for load, passed in self.entry(slot, age, beside):
                    load.wait()
                    passed.wait_recv()
                self.add(self.held.at[slot, age, beside], self.got_core.at[slot, age, beside])
                if beside and slot:
                    self.near(age).start()
                    self.far(age).start()

    def plane(self, age):
        self.near(age).wait_recv()
        self.add(self.held.at[0, age, 1], self.got_near.at[age], self.first)
        self.over_y(age).start()
        self.far(age).wait_recv()
        self.add(self.held.at[1, age, 0], self.got_far.at[age], self.rest)
        self.over_x(age).start()

    def ring(self, age):
        self.over_y(age).wait_recv()
        self.over_x(age).wait_recv()
        if age:
            self.over_z(age - 1).wait_recv()

        def rows_of(index, carry):
            at = pl.ds(pl.multiple_of(index * 16, 16), 16)
            value = self.held[0, age, 0, at, :].astype(F32) + self.got_y[age, at, :].astype(F32)
            value = value + self.got_x[age, at, :].astype(F32)
            if age:
                value = value + self.got_z[age - 1, at, :].astype(F32)
            if age < self.depth - 1:
                self.held[0, age, 0, at, :] = value.astype(BF)
            else:
                for total, column, low, span in self.totals:
                    total[at, column : column + span] = value[:, low : low + span]
            return carry

        lax.fori_loop(0, self.held.shape[3] // 16, rows_of, 0)
        if age < self.depth - 1:
            self.over_z(age).start()

    def finish(self):
        for age in range(self.depth):
            for beside in (1, 0):
                for slot in (1, 0):
                    for _, passed in self.entry(slot, age, beside, False):
                        passed.wait_send()
            for copy in (self.near, self.far, self.over_y, self.over_x):
                copy(age).wait_send()
            if age < self.depth - 1:
                self.over_z(age).wait_send()


def reducer_scratch(size, slot, cut, widths):
    depth = size // 4
    wide = sum(widths)
    sems = pltpu.SemaphoreType.DMA
    return [
        pltpu.VMEM((2, depth, 2, slot, wide), BF),
        pltpu.VMEM((2, depth, 2, slot, wide), BF),
        pltpu.VMEM((depth, slot, cut), BF),
        pltpu.VMEM((depth, slot, wide - cut), BF),
        pltpu.VMEM((depth, slot, wide), BF),
        pltpu.VMEM((depth, slot, wide), BF),
        pltpu.VMEM((depth - 1, slot, wide), BF),
        sems((2, depth, 2, len(widths))),
        sems((2, depth, 2, len(widths), 2)),
        sems((depth, 2)),
        sems((depth, 2)),
        sems((depth, 2)),
        sems((depth, 2)),
        sems((depth - 1, 2)),
    ]


def reduce_kernel(size, cut, widths, *refs):
    pieces = len(widths)
    own, other = refs[:pieces], refs[pieces : 2 * pieces]
    rows_ref = refs[2 * pieces]
    first = 2 * pieces + 1
    totals = refs[first : first + pieces + 2]
    arrived_ref, swap_sem = refs[first + pieces + 2 : first + pieces + 4]
    moves = [
        (total, 0, sum(widths[:index]), widths[index]) for index, total in enumerate(totals[: pieces - 1])
    ]
    base = sum(widths[:-1])
    for lanes in range(widths[-1] // LANES):
        moves.append((totals[pieces - 1 + lanes % 3], lanes // 3 * LANES, base + lanes * LANES, LANES))
    steps = Reducer(size, cut, widths, own, other, moves, refs[first + pieces + 4 :])
    steps.start()
    swapped = steps.remote(rows_ref, arrived_ref, swap_sem, steps.across)
    swapped.start()
    for step in range(steps.depth + 2):
        if step < steps.depth:
            steps.corner(step)
        if 1 <= step <= steps.depth:
            steps.plane(step - 1)
        if step >= 2:
            steps.ring(step - 2)
    swapped.wait_recv()
    swapped.wait_send()
    steps.finish()


def reduce_blocks(own, other, rows, size, cut):
    slot = own[0].shape[0] // size
    widths = tuple(value.shape[1] for value in own)
    blocks = [value.reshape(size, slot, value.shape[1]) for value in (*own, *other)]
    any_spec = pl.BlockSpec(memory_space=pl.ANY)
    *totals, arrived = pl.pallas_call(
        functools.partial(reduce_kernel, size, cut, widths),
        in_specs=[any_spec] * (len(blocks) + 1),
        out_specs=[pl.BlockSpec(memory_space=pltpu.VMEM)] * (len(widths) + 2) + [any_spec],
        out_shape=[jax.ShapeDtypeStruct((slot, width), F32) for width in (*widths[:-1], *[widths[-1] // 3] * 3)]
        + [jax.ShapeDtypeStruct(rows.shape, rows.dtype)],
        scratch_shapes=[pltpu.SemaphoreType.DMA((2,))] + reducer_scratch(size, slot, cut, widths),
        compiler_params=pltpu.CompilerParams(
            collective_id=1, has_side_effects=True, vmem_limit_bytes=VMEM_LIMIT
        ),
        name="reduce_blocks",
    )(*blocks, rows)
    return totals, arrived


PLAN = {
    1: (("corner", 0),),
    2: (("corner", 1), ("corner", 2)),
    3: (("plane", 0), ("corner", 3)),
    4: (("plane", 1),),
    5: (("plane", 2),),
    6: (("plane", 3),),
    7: (("ring", 0),),
    9: (("ring", 1),),
    11: (("ring", 2),),
}


def backward_reduce_kernel(size, cut, widths, flip_ref, bias_ref, *refs):
    own_refs, other_refs = refs[:4], refs[4:8]
    parts = refs[8:12]
    dqkv_ref, outer_ref, inner_ref = refs[12:15]
    work, own_scratch, scratch = refs[15:19], refs[19:24], refs[24:]
    moves = ((outer_ref, 0, 0, widths[0]), (inner_ref, 0, widths[0], widths[1]))
    steps = Reducer(size, cut, widths, parts[:2], parts[2:], moves, scratch)
    at = pl.program_id(0)
    last = pl.num_programs(0) - 1
    pairs = pl.num_programs(0) // 2

    def fill(sources):
        for target, source in zip(work, sources):
            target[...] = source[...]

    @pl.when(at < pairs)
    def _():
        fill(own_refs)

    @pl.when(at >= pairs)
    def _():
        fill(other_refs)

    def hook(head):
        for point, moves in PLAN.items():
            if point % 2 == head:

                @pl.when(at == point // 2)
                def _(moves=moves):
                    for name, age in moves:
                        getattr(steps, name)(age)

    def before():
        @pl.when(at == 0)
        def _():
            steps.start()

        hook(0)

    qkv_ref, grad_ref, out_ref, lse_ref = work
    backward_kernel(
        flip_ref, qkv_ref, bias_ref, grad_ref, out_ref, lse_ref,
        dqkv_ref.at[0], *own_scratch, (before, functools.partial(hook, 1)),
    )

    @pl.when(at == last)
    def _():
        steps.ring(3)
        steps.finish()


def attention_backward_reduce(flips, qkv, bias, grads, outs, lse, own, other, size, cut):
    width = qkv[0].shape[1] // 3
    pairs = width // LANES
    slot = own[0].shape[0] // size
    widths = tuple(value.shape[1] for value in own)
    blocks = [value.reshape(size, slot, value.shape[1]) for value in (*own, *other)]
    any_spec = pl.BlockSpec(memory_space=pl.ANY)

    def half_specs(index):
        return [
            pl.BlockSpec((GROUP_TOK, 3 * LANES), lambda i: (0, index(i))),
            pl.BlockSpec((GROUP_TOK, LANES), lambda i: (0, index(i))),
            pl.BlockSpec((GROUP_TOK, LANES), lambda i: (0, index(i))),
            pl.BlockSpec((1, 8, GROUP_TOK), lambda i: (index(i), 0, 0)),
        ]

    return pl.pallas_call(
        functools.partial(backward_reduce_kernel, size, cut, widths),
        grid=(2 * pairs,),
        in_specs=[
            flip_spec(),
            bias_spec(),
            *half_specs(lambda i: jnp.minimum(i, pairs - 1)),
            *half_specs(lambda i: jnp.maximum(i - pairs, 0)),
            *[any_spec] * 4,
        ],
        out_specs=[
            pl.BlockSpec((1, GROUP_TOK, 3 * LANES), lambda i: (i // pairs, 0, i % pairs)),
            *[pl.BlockSpec((slot, value), lambda i: (0, 0)) for value in widths],
        ],
        out_shape=[
            jax.ShapeDtypeStruct((2, GROUP_TOK, 3 * width), BF),
            *[jax.ShapeDtypeStruct((slot, value), F32) for value in widths],
        ],
        scratch_shapes=[
            pltpu.VMEM((GROUP_TOK, 3 * LANES), BF),
            pltpu.VMEM((GROUP_TOK, LANES), BF),
            pltpu.VMEM((GROUP_TOK, LANES), BF),
            pltpu.VMEM((1, 8, GROUP_TOK), F32),
        ]
        + backward_scratch()
        + reducer_scratch(size, slot, cut, widths),
        compiler_params=pltpu.CompilerParams(
            collective_id=2, has_side_effects=True, vmem_limit_bytes=VMEM_LIMIT
        ),
        name="attention_backward_reduce",
    )(
        jnp.concatenate(flips),
        bias,
        qkv[0], grads[0], outs[0], lse[0],
        qkv[1], grads[1], outs[1], lse[1],
        *blocks,
    )


def swap_pair(value):
    return lax.ppermute(value, "tensor", [(0, 1), (1, 0)])


def swap_bit(value, bit, size):
    return lax.ppermute(value, "dp", [(i, i ^ (1 << bit)) for i in range(size)])


def pick(stacked, index, axis=0):
    return lax.dynamic_index_in_dim(stacked, index, axis, keepdims=False)


def reduce_tree(own, other, order, size, last_type=F32):
    bits = size.bit_length() - 1
    me = lax.axis_index("dp")
    held = [value.reshape((2,) * bits + (value.shape[0] // size,) + value.shape[1:]) for value in (own, other)]
    left = list(range(bits - 1, -1, -1))
    for step, move in enumerate(order):
        kind = last_type if step == len(order) - 1 else own.dtype
        if move == "t":
            arrived = swap_pair(held[1])
            held = [(held[0].astype(F32) + arrived.astype(F32)).astype(kind)]
            continue
        axis = left.index(move)
        left.remove(move)
        mine = lax.rem(lax.div(me, 1 << move), 2)
        arrived = [swap_bit(pick(value, 1 - mine, axis), move, size) for value in held]
        held = [
            (pick(value, mine, axis).astype(F32) + got.astype(F32)).astype(kind)
            for value, got in zip(held, arrived)
        ]
    return held[0]


def tree_order(size, pair_first):
    bits = size.bit_length() - 1
    rest = list(range(bits - 1, 1, -1))
    if pair_first:
        return [0, "t", 1] + rest
    return [0, 1, "t"] + rest


def local(
    inputs,
    cotangent,
    seg_ids,
    block_perm,
    query_weight,
    key_weight,
    value_weight,
    output_weight,
    inner_weight,
    outer_weight,
    first_gain,
    first_shift,
    second_gain,
    second_shift,
    size,
):
    rank = lax.axis_index("tensor")
    at_first = rank == 0

    def both(stacked):
        return pick(stacked, rank), pick(stacked, 1 - rank)

    width = query_weight.shape[1]
    hidden_width = inner_weight.shape[1]
    slot = query_weight.shape[0]
    vectors = jnp.concatenate([first_gain, first_shift, second_gain, second_shift])
    per_vector = first_gain.shape[0]
    order = block_perm.reshape(-1).astype(BF)
    vector_block = jnp.concatenate(
        [jnp.pad(value[None, :], ((0, 0), (0, 128 - value.shape[0]))) for value in (vectors, order)]
        + [jnp.zeros((slot - 2, 128), BF)]
    )
    pieces = [query_weight, key_weight, value_weight, output_weight.T, vector_block, inner_weight, outer_weight.T]
    plan = [
        [(pair * LANES, (3 * pair + index) * LANES, LANES) for pair in range(width // LANES)] for index in range(3)
    ]
    reached = 3 * width
    for piece in pieces[3:]:
        plan.append([(0, reached, piece.shape[1])])
        reached += piece.shape[1]
    own, other, arrived_rows = gather_weights(pieces, plan, inputs, size)
    flat = [value.reshape(-1, value.shape[-1]) for value in (own, other)]
    edges = [0, 3 * width, 4 * width, 4 * width + 128, 4 * width + 128 + hidden_width, reached]
    w_qkv, w_output, vector_rows, w_inner, w_outer = [
        [value[:, low:high] for value in flat] for low, high in zip(edges[:-1], edges[1:])
    ]
    perms = [value[1, : order.shape[0]].astype(jnp.int32).reshape(block_perm.shape) for value in vector_rows]
    vector_rows = [value.reshape(size, slot, 128)[:, 0, : 4 * per_vector] for value in vector_rows]
    all_vectors = jnp.stack(
        [jnp.where(at_first, *vector_rows), jnp.where(at_first, *vector_rows[::-1])], axis=1
    )
    all_vectors = all_vectors.reshape(size, 2, 4, per_vector).transpose(2, 0, 1, 3).reshape(4, -1)
    gain_one, shift_one, gain_two, shift_two = [all_vectors[i].astype(F32) for i in range(4)]

    def collect(mine_and_other, arrived):
        mine = pick(mine_and_other, rank)
        return jnp.concatenate(
            [jnp.where(at_first, mine, arrived), jnp.where(at_first, arrived, mine)], axis=0
        )

    def spread(rows, arrived=None):
        halves = rows.reshape((2, rows.shape[0] // 2) + rows.shape[1:])
        mine = pick(halves, rank)
        if arrived is None:
            arrived = swap_pair(pick(halves, 1 - rank).astype(BF))
        arrived = arrived.astype(rows.dtype)
        return jnp.stack([jnp.where(at_first, mine, arrived), jnp.where(at_first, arrived, mine)])

    rows = collect(inputs, arrived_rows)
    segments = pick(seg_ids, rank)[0]
    bias = jnp.where(segments[:, None] == segments[None, :], 0.0, MASKED).astype(F32)

    qkv = [matmul(rows, weight).astype(BF) for weight in w_qkv]
    qkv[0], late = lax.optimization_barrier((qkv[0], pick(cotangent, 1 - rank)))
    late = swap_pair(late)
    attended, lse = zip(*[attention_forward(p, value, bias) for p, value in zip(perms, qkv)])
    attention_sum = contract_cols(attended[0], w_output[0]) + contract_cols(attended[1], w_output[1])
    attention_sum, late = lax.optimization_barrier((attention_sum, late))
    upstream = collect(cotangent, late).astype(F32)
    hidden, unit_one, inverse_one = normalize(rows.astype(F32) + attention_sum, gain_one, shift_one)
    hidden_low = hidden.astype(BF)
    activated, slope = zip(*[gelu_pair(matmul(hidden_low, weight)) for weight in w_inner])
    activated = [value.astype(BF) for value in activated]
    slope = [value.astype(BF) for value in slope]
    branch = contract_cols(activated[0], w_outer[0]) + contract_cols(activated[1], w_outer[1])
    layer_out, unit_two, inverse_two = normalize(hidden + branch, gain_two, shift_two)
    layer_low = layer_out.astype(BF)
    layer_leaving = pick(layer_low.reshape(4, -1, layer_low.shape[1]).reshape(2, 2, -1, layer_low.shape[1]), 1 - rank)
    layer_first = swap_pair(layer_leaving[0])

    second_back = normalize_back(upstream, unit_two, inverse_two, gain_two)
    branch_grad = second_back.astype(BF)
    outer_terms = [contract_rows(branch_grad, value).astype(BF) for value in activated]
    pre_grad = [
        (matmul(branch_grad, weight) * part.astype(F32)).astype(BF) for weight, part in zip(w_outer, slope)
    ]
    layer_first, pre_grad[1] = lax.optimization_barrier((layer_first, pre_grad[1]))
    layer_second, layer_first = lax.optimization_barrier((layer_leaving[1], layer_first))
    layer_second = swap_pair(layer_second)
    inner_terms = [contract_rows(hidden_low, value).astype(BF) for value in pre_grad]
    hidden_back = second_back + contract_cols(pre_grad[0], w_inner[0]) + contract_cols(pre_grad[1], w_inner[1])
    first_back = normalize_back(hidden_back, unit_one, inverse_one, gain_one)
    norm_terms = jnp.stack(
        [
            jnp.sum(hidden_back * unit_one, axis=0),
            jnp.sum(hidden_back, axis=0),
            jnp.sum(upstream * unit_two, axis=0),
            jnp.sum(upstream, axis=0),
        ]
    )
    by_shard = norm_terms.reshape(4, size, 2, per_vector).transpose(2, 1, 0, 3).reshape(2, size, 4, per_vector)
    vector_terms = [
        jnp.pad(value.reshape(size, 1, 4 * per_vector), ((0, 0), (0, slot - 1), (0, 128 - 4 * per_vector)))
        .reshape(size * slot, 128)
        .astype(BF)
        for value in both(by_shard)
    ]

    attention_grad = first_back.astype(BF)
    output_terms = [contract_rows(attention_grad, value).astype(BF) for value in attended]
    attended_grad = [matmul(attention_grad, weight).astype(BF) for weight in w_output]
    layer_second, attended_grad[0] = lax.optimization_barrier((layer_second, attended_grad[0]))
    layer_arrived = jnp.concatenate([layer_first, layer_second])
    layer_rows = spread(layer_low, layer_arrived)
    flips = [
        jnp.broadcast_to(
            jnp.pad(value[:, 0].astype(F32).reshape(-1, 2), ((0, 0), (0, 6)))[:, :, None],
            (value.shape[0] // 2, 8, HALF),
        )
        for value in perms
    ]
    fast = size == 16 and slot % 16 == 0
    if fast:
        head_grads, grad_outer, grad_inner = attention_backward_reduce(
            flips, qkv, bias, attended_grad, attended, lse, *zip(outer_terms, inner_terms), size, BACK_CUT
        )
    else:
        operands = zip(flips, qkv, [bias] * 2, attended_grad, attended, lse)
        head_grads = [attention_backward(*values) for values in operands]
    head_terms = [contract_rows(rows, value).astype(BF) for value in head_grads]
    input_grad = first_back + contract_cols(head_grads[0], w_qkv[0]) + contract_cols(head_grads[1], w_qkv[1])
    def put(rows_out, value, index):
        return lax.dynamic_update_slice(rows_out, value[None], (index, 0, 0))

    halves = input_grad.reshape(2, GROUP_TOK // 2, -1)
    leaving = pick(halves, 1 - rank).astype(BF)
    terms = list(zip(output_terms, vector_terms, head_terms))
    if fast:
        (grad_output, norm_rows, grad_query, grad_key, grad_value), arrived = reduce_blocks(
            *terms, leaving, size, REDUCE_CUT
        )
    else:
        terms = [(outer, inner, *rest) for outer, inner, rest in zip(outer_terms, inner_terms, terms)]
        packed = [jnp.concatenate(value, axis=1) for value in terms]
        total, arrived = reduce_tree(*packed, tree_order(size, True), size), swap_pair(leaving)
        total = total.reshape(slot, -1)
        edges = [0]
        for value in terms[0]:
            edges.append(edges[-1] + value.shape[1])
        grad_outer, grad_inner, grad_output, norm_rows, grad_heads = [
            total[:, low:high] for low, high in zip(edges[:-1], edges[1:])
        ]
        grad_heads = grad_heads.reshape(slot, -1, 3, LANES)
        grad_query, grad_key, grad_value = [grad_heads[:, :, i].reshape(slot, width) for i in range(3)]
    input_rows = put(put(jnp.zeros_like(halves), pick(halves, rank), rank), arrived.astype(F32), 1 - rank)
    norm_shards = norm_rows[0, : 4 * per_vector].reshape(4, per_vector)
    return (
        layer_rows,
        input_rows,
        grad_query,
        grad_key,
        grad_value,
        grad_output.T,
        grad_inner,
        grad_outer.T,
        norm_shards[0],
        norm_shards[1],
        norm_shards[2],
        norm_shards[3],
    )


def solution(mesh):
    rows = P(None, ("dp", "tensor"), None)
    columns = P("dp", "tensor")
    flipped = P("tensor", "dp")
    vector = P(("dp", "tensor"))
    return jax.shard_map(
        functools.partial(local, size=mesh.shape["dp"]),
        mesh=mesh,
        in_specs=(
            rows, rows, P(None, "dp", None), P("tensor", None),
            columns, columns, columns, flipped, columns, flipped,
            vector, vector, vector, vector,
        ),
        out_specs=(
            rows, rows, columns, columns, columns, flipped, columns, flipped,
            vector, vector, vector, vector,
        ),
        check_vma=False,
    )
```

```python
import functools
import math

import jax
import jax.numpy as jnp
from jax import lax
from jax.experimental import pallas as pl
from jax.experimental.pallas import tpu as pltpu
from jax.sharding import PartitionSpec as P

HEAD_WIDTH = 64
PROMPT_LENGTH = 512
CONT_TOK = 512
GROUP_TOK = PROMPT_LENGTH + CONT_TOK
HALF = PROMPT_LENGTH // 2
LANES = 2 * HEAD_WIDTH
CHUNK = 256

EPSILON = 1e-05
MASKED = -1e30
SCALE = 1.0 / math.sqrt(HEAD_WIDTH)
ROOT_HALF = 1.0 / math.sqrt(2.0)
ROOT_TWO_PI = 1.0 / math.sqrt(2.0 * math.pi)


BF = jnp.bfloat16
F32 = jnp.float32


def dot(left, right, dims):
    return lax.dot_general(left, right, (dims, ((), ())), preferred_element_type=F32)


def matmul(left, right):
    return dot(left, right, ((1,), (0,)))


def contract_rows(left, right):
    return dot(left, right, ((0,), (0,)))


def contract_cols(left, right):
    return dot(left, right, ((1,), (1,)))


def normalize(residual, gain_vector, shift_vector):
    centred = residual - jnp.mean(residual, axis=-1, keepdims=True)
    inverse = lax.rsqrt(jnp.mean(centred * centred, axis=-1, keepdims=True) + EPSILON)
    unit_rows = centred * inverse
    return (unit_rows * gain_vector + shift_vector, unit_rows, inverse)


def normalize_back(upstream, unit_rows, inverse, gain_vector):
    scaled = upstream * gain_vector
    first_mean = jnp.mean(scaled, axis=-1, keepdims=True)
    second_mean = jnp.mean(scaled * unit_rows, axis=-1, keepdims=True)
    return inverse * (scaled - first_mean - unit_rows * second_mean)


def gelu_pair(values):
    normal_cdf = 0.5 * (1.0 + lax.erf(values * ROOT_HALF))
    density = jnp.exp(-0.5 * values * values) * ROOT_TWO_PI
    return (values * normal_cdf, normal_cdf + values * density)


def head_lanes(head, value):
    lane = lax.broadcasted_iota(jnp.int32, value.shape, 1)
    return jnp.where((lane // HEAD_WIDTH) == head, value, jnp.zeros_like(value))


def thirds(ref):
    return [ref.at[:, i * LANES : (i + 1) * LANES] for i in range(3)]


def forward_kernel(perm_ref, qkv_ref, bias_ref, out_ref, lse_ref, vt_ref, ot_ref):
    pair = pl.program_id(0)
    q_ref, k_ref, v_ref = thirds(qkv_ref)
    vt_ref[...] = v_ref[...].T
    for head in range(2):
        lanes = slice(head * HEAD_WIDTH, (head + 1) * HEAD_WIDTH)

        def finish(scores, values_t, columns):
            top = jnp.max(scores, axis=0, keepdims=True)
            weights = jnp.exp(scores - top)
            total = jnp.sum(weights, axis=0, keepdims=True)
            out_t = matmul(values_t, weights.astype(BF))
            ot_ref[lanes, columns] = out_t / total
            lse_ref[0, head : head + 1, columns] = top + jnp.log(total)

        for block in range(2):
            columns = slice(block * HALF, (block + 1) * HALF)
            start = pl.multiple_of(perm_ref[pair * 2 + head, block] * HALF, HALF)
            queries = head_lanes(head, q_ref[columns, :]) * SCALE
            scores = contract_cols(k_ref[pl.ds(start, HALF), :], queries.astype(BF))
            finish(scores, vt_ref[lanes, pl.ds(start, HALF)], columns)
        for chunk in range(CONT_TOK // CHUNK):
            first = PROMPT_LENGTH + chunk * CHUNK
            columns = slice(first, first + CHUNK)
            queries = (head_lanes(head, q_ref[columns, :]) * SCALE).astype(BF)
            scores = jnp.concatenate(
                [
                    contract_cols(k_ref[:PROMPT_LENGTH, :], queries),
                    contract_cols(k_ref[PROMPT_LENGTH:, :], queries)
                    + bias_ref[:, chunk * CHUNK : (chunk + 1) * CHUNK],
                ],
                axis=0,
            )
            finish(scores, vt_ref[lanes, :], columns)
    out_ref[...] = ot_ref[...].T.astype(BF)


def backward_kernel(
    flip_ref, qkv_ref, bias_ref, grad_ref, out_ref, lse_ref,
    dqkv_ref, kt_ref, dqt_ref, dka_ref, dva_ref, delta_ref, hooks=(),
):
    q_ref, k_ref, v_ref = thirds(qkv_ref)
    dq_ref, dk_ref, dv_ref = thirds(dqkv_ref)
    kt_ref[...] = k_ref[...].T
    product = (grad_ref[...].astype(F32) * out_ref[...].astype(F32)).T
    for head in range(2):
        lanes = slice(head * HEAD_WIDTH, (head + 1) * HEAD_WIDTH)
        delta_ref[head : head + 1, :] = jnp.sum(product[lanes, :], axis=0, keepdims=True)
    for head in range(2):
        if hooks:
            hooks[head]()
        lanes = slice(head * HEAD_WIDTH, (head + 1) * HEAD_WIDTH)

        def score_grad(scores, values, grads, columns):
            probs = jnp.exp(scores - lse_ref[0, head : head + 1, columns])
            prob_grad = contract_cols(values, grads)
            grad_scores = probs * (prob_grad - delta_ref[head : head + 1, columns])
            return probs.astype(BF), grad_scores.astype(BF)

        for chunk in range(CONT_TOK // CHUNK):
            first = PROMPT_LENGTH + chunk * CHUNK
            columns = slice(first, first + CHUNK)
            queries = (head_lanes(head, q_ref[columns, :]) * SCALE).astype(BF)
            grads = head_lanes(head, grad_ref[columns, :])
            scores = jnp.concatenate(
                [
                    contract_cols(k_ref[:PROMPT_LENGTH, :], queries),
                    contract_cols(k_ref[PROMPT_LENGTH:, :], queries)
                    + bias_ref[:, chunk * CHUNK : (chunk + 1) * CHUNK],
                ],
                axis=0,
            )
            probs, grad_scores = score_grad(scores, v_ref[...], grads, columns)
            dqt_ref[lanes, columns] = matmul(kt_ref[lanes, :], grad_scores) * SCALE
            key_part = matmul(grad_scores, queries)
            value_part = matmul(probs, grads)
            if head == 0 and chunk == 0:
                dka_ref[...] = key_part
                dva_ref[...] = value_part
            else:
                dka_ref[...] += key_part
                dva_ref[...] += value_part
        flip = flip_ref[0, head : head + 1, :] > 0.5
        narrow = flip[:, :LANES]

        def choose(mask, straight, crossed, block):
            return jnp.where(mask, crossed, straight) if block == 0 else jnp.where(mask, straight, crossed)

        key_parts, value_parts = [], []
        for block in range(2):
            columns = slice(block * HALF, (block + 1) * HALF)
            keys = choose(narrow, k_ref[:HALF, :], k_ref[HALF:PROMPT_LENGTH, :], block)
            values = choose(narrow, v_ref[:HALF, :], v_ref[HALF:PROMPT_LENGTH, :], block)
            keys_t = choose(flip, kt_ref[lanes, :HALF], kt_ref[lanes, HALF:PROMPT_LENGTH], block)
            queries = (head_lanes(head, q_ref[columns, :]) * SCALE).astype(BF)
            grads = head_lanes(head, grad_ref[columns, :])
            scores = contract_cols(keys, queries)
            probs, grad_scores = score_grad(scores, values, grads, columns)
            dqt_ref[lanes, columns] = matmul(keys_t, grad_scores) * SCALE
            key_parts.append(matmul(grad_scores, queries))
            value_parts.append(matmul(probs, grads))
        for total_ref, (one, two) in ((dka_ref, key_parts), (dva_ref, value_parts)):
            total_ref[:HALF, :] += choose(narrow, one, two, 0)
            total_ref[HALF:PROMPT_LENGTH, :] += choose(narrow, one, two, 1)
    dq_ref[...] = dqt_ref[...].T.astype(BF)
    dk_ref[...] = dka_ref[...].astype(BF)
    dv_ref[...] = dva_ref[...].astype(BF)


GATHER_CUT = 640
LATE = 1408
LATE_CUT = 640
REDUCE_CUT = 128
BACK_CUT = 1536
VMEM_LIMIT = 56 * 1024 * 1024


def column_spec(lanes):
    return pl.BlockSpec((GROUP_TOK, lanes), lambda i: (0, i))


def flip_spec():
    return pl.BlockSpec((1, 8, HALF), lambda i: (i, 0, 0))


def bias_spec():
    return pl.BlockSpec((CONT_TOK, CONT_TOK), lambda i: (0, 0))


def lse_spec():
    return pl.BlockSpec((1, 8, GROUP_TOK), lambda i: (i, 0, 0))


def attention_forward(perm, qkv, bias):
    width = qkv.shape[1] // 3
    pairs = width // LANES
    return pl.pallas_call(
        forward_kernel,
        grid=(pairs,),
        in_specs=[
            pl.BlockSpec(memory_space=pltpu.SMEM),
            column_spec(3 * LANES),
            bias_spec(),
        ],
        out_specs=[column_spec(LANES), lse_spec()],
        out_shape=[
            jax.ShapeDtypeStruct((GROUP_TOK, width), BF),
            jax.ShapeDtypeStruct((pairs, 8, GROUP_TOK), F32),
        ],
        scratch_shapes=[
            pltpu.VMEM((LANES, GROUP_TOK), BF),
            pltpu.VMEM((LANES, GROUP_TOK), F32),
        ],
        compiler_params=pltpu.CompilerParams(vmem_limit_bytes=VMEM_LIMIT),
        cost_estimate=pl.CostEstimate(
            flops=pairs * 8 * 655360 * 256, bytes_accessed=4 * GROUP_TOK * width * 2, transcendentals=0
        ),
        name="attention_forward",
    )(perm, qkv, bias)


def backward_scratch():
    return [
        pltpu.VMEM((LANES, GROUP_TOK), BF),
        pltpu.VMEM((LANES, GROUP_TOK), F32),
        pltpu.VMEM((GROUP_TOK, LANES), F32),
        pltpu.VMEM((GROUP_TOK, LANES), F32),
        pltpu.VMEM((8, GROUP_TOK), F32),
    ]


def attention_backward(flip, qkv, bias, grads, outs, lse):
    width = qkv.shape[1] // 3
    pairs = width // LANES
    return pl.pallas_call(
        backward_kernel,
        grid=(pairs,),
        in_specs=[
            flip_spec(),
            column_spec(3 * LANES),
            bias_spec(),
            column_spec(LANES),
            column_spec(LANES),
            lse_spec(),
        ],
        out_specs=column_spec(3 * LANES),
        out_shape=jax.ShapeDtypeStruct((GROUP_TOK, 3 * width), BF),
        scratch_shapes=backward_scratch(),
        compiler_params=pltpu.CompilerParams(vmem_limit_bytes=VMEM_LIMIT),
        cost_estimate=pl.CostEstimate(
            flops=pairs * 20 * 655360 * 256, bytes_accessed=8 * GROUP_TOK * width * 2, transcendentals=0
        ),
        name="attention_backward",
    )(flip, qkv, bias, grads, outs, lse)


def gather_kernel(
    size, plan, places, *refs,
):
    pieces = refs[: len(plan)]
    inputs_ref, own_ref, other_ref, arrived_ref, shard_ref = refs[len(plan) : len(plan) + 5]
    (
        load_sem, local_sem, swap_sem, z_sem, y_sem, x_sem, near_sem, far_sem, core_sem,
        late_z, late_y, late_x, late_near, late_far, late_core,
    ) = refs[len(plan) + 5 :]
    cut, base, late_cut, wide = places
    loads = []
    for piece, moves in zip(pieces, plan):
        for source, landing, width in moves:
            load = pltpu.make_async_copy(
                piece.at[:, source : source + width],
                shard_ref.at[:, landing : landing + width],
                load_sem.at[len(loads)],
            )
            load.start()
            loads.append(load)
    depth = size // 4
    me = lax.axis_index("dp")
    rank = lax.axis_index("tensor")
    z = lax.div(me, 4)
    y = lax.rem(lax.div(me, 2), 2)
    core = lax.rem(me, 2)

    def place(zz, yy, cc):
        return zz * 4 + yy * 2 + cc

    up = {"dp": place(lax.rem(z + 1, depth), y, core)}
    down = {"dp": place(lax.rem(z + depth - 1, depth), y, core)}
    side = {"dp": place(z, 1 - y, core)}
    twin = {"dp": place(z, y, 1 - core)}
    across = {"tensor": 1 - rank}

    barrier = pltpu.get_barrier_semaphore()
    for target in (up, down, side, twin, across):
        pl.semaphore_signal(barrier, inc=1, device_id=target, device_id_type=pl.DeviceIdType.MESH)
    pl.semaphore_wait(barrier, 5)

    started = []

    def send(source, landing, sems, target):
        copy = pltpu.make_async_remote_copy(
            src_ref=source,
            dst_ref=landing,
            send_sem=sems.at[0],
            recv_sem=sems.at[1],
            device_id=target,
            device_id_type=pl.DeviceIdType.MESH,
        )
        copy.start()
        started.append(copy)

    def receive(landing, sems, target):
        pltpu.make_async_remote_copy(
            src_ref=landing,
            dst_ref=landing,
            send_sem=sems.at[0],
            recv_sem=sems.at[1],
            device_id=target,
            device_id_type=pl.DeviceIdType.MESH,
        ).wait_recv()

    for load in loads:
        load.wait()
    keep = pltpu.make_async_copy(shard_ref, own_ref.at[me], local_sem)
    keep.start()

    def slots(age):
        zz = lax.rem(z - age + depth, depth)
        return place(zz, y, core), place(zz, 1 - y, core)

    early = slice(0, base)
    late = slice(base, wide)
    first, rest = slice(0, cut), slice(cut, base)
    late_first, late_rest = slice(base, late_cut), slice(late_cut, wide)

    def late_block(kind, age, columns=late):
        half = own_ref if kind < 2 else other_ref
        return half.at[slots(age)[kind % 2], :, columns]

    def pass_late(kind, age, block=None):
        landing = late_block(kind, age)
        block = landing if block is None else block
        if age < depth - 1:
            send(block, landing, late_z.at[kind, age], up)
        send(block, landing, late_core.at[kind, age], twin)

    for step in range(depth + 2):
        if step < depth:
            mine, _ = slots(step)
            landing = own_ref.at[mine, :, early]
            if step == 0:
                block = shard_ref.at[:, early]
            else:
                block = landing
                receive(block, z_sem.at[step - 1], up)
            if step < depth - 1:
                send(block, landing, z_sem.at[step], up)
            if step == 0:
                send(shard_ref.at[:, late], late_block(0, 0), late_y, side)
                send(shard_ref.at[:, late], late_block(2, 0), late_x, across)
                pass_late(0, 0, shard_ref.at[:, late])
            send(block, landing, y_sem.at[step], side)
            send(block, other_ref.at[mine, :, early], x_sem.at[step], across)
            send(block, landing, core_sem.at[0, step], twin)
            if step == 0:
                send(inputs_ref.at[1 - rank], arrived_ref, swap_sem, across)
        if step == 1:
            receive(late_block(1, 0), late_y, side)
            send(late_block(1, 0, late_first), late_block(3, 0, late_first), late_near, across)
            pass_late(1, 0)
            receive(late_block(2, 0), late_x, across)
            mine, _ = slots(0)
            send(other_ref.at[mine, :, late_rest], other_ref.at[mine, :, late_rest], late_far, side)
            pass_late(2, 0)
        if 2 <= step <= depth:
            for kind in range(3):
                receive(late_block(kind, step - 1), late_z.at[kind, step - 2], up)
                pass_late(kind, step - 1)
        if step >= 2:
            if step == 2:
                receive(late_block(3, 0, late_first), late_near, across)
                receive(late_block(3, 0, late_rest), late_far, side)
            else:
                receive(late_block(3, step - 2), late_z.at[3, step - 3], up)
            pass_late(3, step - 2)
        if 1 <= step <= depth:
            age = step - 1
            mine, beside = slots(age)
            block = own_ref.at[beside, :, early]
            receive(block, y_sem.at[age], side)
            send(own_ref.at[beside, :, first], other_ref.at[beside, :, first], near_sem.at[age], across)
            send(block, block, core_sem.at[1, age], twin)
            block = other_ref.at[mine, :, early]
            receive(block, x_sem.at[age], across)
            send(other_ref.at[mine, :, rest], other_ref.at[mine, :, rest], far_sem.at[age], side)
            send(block, block, core_sem.at[2, age], twin)
        if step >= 2:
            age = step - 2
            _, beside = slots(age)
            receive(other_ref.at[beside, :, first], near_sem.at[age], across)
            receive(other_ref.at[beside, :, rest], far_sem.at[age], side)
            block = other_ref.at[beside, :, early]
            send(block, block, core_sem.at[3, age], twin)
    receive(arrived_ref, swap_sem, across)
    for age in range(depth):
        zz = lax.rem(z - age + depth, depth)
        here, there = place(zz, y, 1 - core), place(zz, 1 - y, 1 - core)
        blocks = (own_ref.at[here], own_ref.at[there], other_ref.at[here], other_ref.at[there])
        for kind, block in enumerate(blocks):
            receive(block.at[:, early], core_sem.at[kind, age], twin)
            receive(block.at[:, late], late_core.at[kind, age], twin)
    for copy in started:
        copy.wait_send()
    keep.wait()


def gather_weights(pieces, plan, inputs, size):
    depth = size // 4
    slot = pieces[0].shape[0]
    moves = [move for piece in plan for move in piece]
    wide = sum(width for _, _, width in moves)
    whole = jax.ShapeDtypeStruct((size, slot, wide), BF)
    sems = pltpu.SemaphoreType.DMA
    base = wide - LATE
    return pl.pallas_call(
        functools.partial(gather_kernel, size, plan, (GATHER_CUT, base, base + LATE_CUT, wide)),
        in_specs=[pl.BlockSpec(memory_space=pl.ANY)] * (len(pieces) + 1),
        out_specs=[pl.BlockSpec(memory_space=pl.ANY)] * 3,
        out_shape=[whole, whole, jax.ShapeDtypeStruct(inputs.shape[1:], inputs.dtype)],
        scratch_shapes=[
            pltpu.VMEM((slot, wide), BF),
            sems((len(moves),)),
            sems,
            sems((2,)),
            sems((depth - 1, 2)),
            sems((depth, 2)),
            sems((depth, 2)),
            sems((depth, 2)),
            sems((depth, 2)),
            sems((4, depth, 2)),
            sems((4, depth - 1, 2)),
            sems((2,)),
            sems((2,)),
            sems((2,)),
            sems((2,)),
            sems((4, depth, 2)),
        ],
        compiler_params=pltpu.CompilerParams(collective_id=0, has_side_effects=True),
        name="gather_weights",
    )(*pieces, inputs)


class Reducer:
    def __init__(self, size, cut, widths, own, other, totals, scratch):
        (
            self.held, self.got_core, self.got_near, self.got_far, self.got_y, self.got_x, self.got_z,
            self.load_sem, self.core_sem, self.near_sem, self.far_sem, self.y_sem, self.x_sem, self.z_sem,
        ) = scratch
        self.parts = (own, other)
        self.totals = totals
        self.first = slice(0, cut)
        self.rest = slice(cut, sum(widths))
        self.edges = [sum(widths[:i]) for i in range(len(widths) + 1)]
        self.depth = size // 4
        me = lax.axis_index("dp")
        self.z = lax.div(me, 4)
        self.y = lax.rem(lax.div(me, 2), 2)
        self.core = lax.rem(me, 2)
        z, y, core, depth = self.z, self.y, self.core, self.depth
        self.up = {"dp": self.place(lax.rem(z + 1, depth), y, core)}
        self.down = {"dp": self.place(lax.rem(z + depth - 1, depth), y, core)}
        self.side = {"dp": self.place(z, 1 - y, core)}
        self.twin = {"dp": self.place(z, y, 1 - core)}
        self.across = {"tensor": 1 - lax.axis_index("tensor")}

    @staticmethod
    def place(zz, yy, cc):
        return zz * 4 + yy * 2 + cc

    def greet(self):
        barrier = pltpu.get_barrier_semaphore()
        for target in (self.up, self.down, self.side, self.twin, self.across):
            pl.semaphore_signal(barrier, inc=1, device_id=target, device_id_type=pl.DeviceIdType.MESH)
        pl.semaphore_wait(barrier, 5)

    @staticmethod
    def remote(source, landing, sems, target):
        return pltpu.make_async_remote_copy(
            src_ref=source,
            dst_ref=landing,
            send_sem=sems.at[0],
            recv_sem=sems.at[1],
            device_id=target,
            device_id_type=pl.DeviceIdType.MESH,
        )

    def entry(self, slot, age, beside, loads=True):
        zz = lax.rem(self.z + 2 * self.depth - 1 - age, self.depth)
        yy = 1 - self.y if beside else self.y
        copies = []
        for index, source in enumerate(self.parts[slot]):
            columns = slice(self.edges[index], self.edges[index + 1])
            passed = self.remote(
                source.at[self.place(zz, yy, 1 - self.core)],
                self.got_core.at[slot, age, beside, :, columns],
                self.core_sem.at[slot, age, beside, index],
                self.twin,
            )
            load = None
            if loads:
                load = pltpu.make_async_copy(
                    source.at[self.place(zz, yy, self.core)],
                    self.held.at[slot, age, beside, :, columns],
                    self.load_sem.at[slot, age, beside, index],
                )
            copies.append((load, passed))
        return copies

    def near(self, age):
        return self.remote(
            self.held.at[1, age, 1, :, self.first], self.got_near.at[age], self.near_sem.at[age], self.across
        )

    def far(self, age):
        return self.remote(
            self.held.at[1, age, 1, :, self.rest], self.got_far.at[age], self.far_sem.at[age], self.side
        )

    def over_y(self, age):
        return self.remote(self.held.at[0, age, 1], self.got_y.at[age], self.y_sem.at[age], self.side)

    def over_x(self, age):
        return self.remote(self.held.at[1, age, 0], self.got_x.at[age], self.x_sem.at[age], self.across)

    def over_z(self, age):
        return self.remote(self.held.at[0, age, 0], self.got_z.at[age], self.z_sem.at[age], self.up)

    @staticmethod
    def add(target, addend, columns=slice(None)):
        def rows_of(index, carry):
            at = pl.ds(pl.multiple_of(index * 16, 16), 16)
            target[at, columns] = (target[at, columns].astype(F32) + addend[at, :].astype(F32)).astype(BF)
            return carry

        lax.fori_loop(0, target.shape[0] // 16, rows_of, 0)

    def start(self):
        self.greet()
        for age in range(self.depth):
            for beside in (1, 0):
                for slot in (1, 0):
                    for load, passed in self.entry(slot, age, beside):
                        passed.start()
                        load.start()

    def corner(self, age):
        for beside in (1, 0):
            for slot in (1, 0):
                for load, passed in self.entry(slot, age, beside):
                    load.wait()
                    passed.wait_recv()
                self.add(self.held.at[slot, age, beside], self.got_core.at[slot, age, beside])
                if beside and slot:
                    self.near(age).start()
                    self.far(age).start()

    def plane(self, age):
        self.near(age).wait_recv()
        self.add(self.held.at[0, age, 1], self.got_near.at[age], self.first)
        self.over_y(age).start()
        self.far(age).wait_recv()
        self.add(self.held.at[1, age, 0], self.got_far.at[age], self.rest)
        self.over_x(age).start()

    def ring(self, age):
        self.over_y(age).wait_recv()
        self.over_x(age).wait_recv()
        if age:
            self.over_z(age - 1).wait_recv()

        def rows_of(index, carry):
            at = pl.ds(pl.multiple_of(index * 16, 16), 16)
            value = self.held[0, age, 0, at, :].astype(F32) + self.got_y[age, at, :].astype(F32)
            value = value + self.got_x[age, at, :].astype(F32)
            if age:
                value = value + self.got_z[age - 1, at, :].astype(F32)
            if age < self.depth - 1:
                self.held[0, age, 0, at, :] = value.astype(BF)
            else:
                for total, column, low, span in self.totals:
                    total[at, column : column + span] = value[:, low : low + span]
            return carry

        lax.fori_loop(0, self.held.shape[3] // 16, rows_of, 0)
        if age < self.depth - 1:
            self.over_z(age).start()

    def finish(self):
        for age in range(self.depth):
            for beside in (1, 0):
                for slot in (1, 0):
                    for _, passed in self.entry(slot, age, beside, False):
                        passed.wait_send()
            for copy in (self.near, self.far, self.over_y, self.over_x):
                copy(age).wait_send()
            if age < self.depth - 1:
                self.over_z(age).wait_send()


def reducer_scratch(size, slot, cut, widths):
    depth = size // 4
    wide = sum(widths)
    sems = pltpu.SemaphoreType.DMA
    return [
        pltpu.VMEM((2, depth, 2, slot, wide), BF),
        pltpu.VMEM((2, depth, 2, slot, wide), BF),
        pltpu.VMEM((depth, slot, cut), BF),
        pltpu.VMEM((depth, slot, wide - cut), BF),
        pltpu.VMEM((depth, slot, wide), BF),
        pltpu.VMEM((depth, slot, wide), BF),
        pltpu.VMEM((depth - 1, slot, wide), BF),
        sems((2, depth, 2, len(widths))),
        sems((2, depth, 2, len(widths), 2)),
        sems((depth, 2)),
        sems((depth, 2)),
        sems((depth, 2)),
        sems((depth, 2)),
        sems((depth - 1, 2)),
    ]


def reduce_kernel(size, cut, widths, *refs):
    pieces = len(widths)
    own, other = refs[:pieces], refs[pieces : 2 * pieces]
    head_ref, own_weight, other_weight, back_ref = refs[2 * pieces : 2 * pieces + 4]
    first = 2 * pieces + 4
    totals = refs[first : first + pieces + 2]
    arrived_ref, mine_ref, swap_sem, load_sem, heads, weights, leaving = refs[first + pieces + 2 : first + pieces + 9]
    moves = [
        (total, 0, sum(widths[:index]), widths[index]) for index, total in enumerate(totals[: pieces - 1])
    ]
    base = sum(widths[:-1])
    for lanes in range(widths[-1] // LANES):
        moves.append((totals[pieces - 1 + lanes % 3], lanes // 3 * LANES, base + lanes * LANES, LANES))
    steps = Reducer(size, cut, widths, own, other, moves, refs[first + pieces + 9 :])
    columns = slice(0, widths[-1])
    loads = [
        pltpu.make_async_copy(head_ref, heads, load_sem.at[0]),
        pltpu.make_async_copy(own_weight.at[:, columns], weights.at[0], load_sem.at[1]),
        pltpu.make_async_copy(other_weight.at[:, columns], weights.at[1], load_sem.at[2]),
    ]
    for load in loads:
        load.start()
    steps.start()
    rank = lax.axis_index("tensor")
    count = leaving.shape[0]

    def input_rows(start, target):
        def some(index, carry):
            at = pl.ds(pl.multiple_of(start + index * CHUNK, CHUNK), CHUNK)
            value = back_ref[at, :]
            for half in range(2):
                value = value + contract_cols(heads[half, at, :], weights[half])
            target[pl.ds(pl.multiple_of(index * CHUNK, CHUNK), CHUNK), :] = value.astype(target.dtype)
            return carry

        lax.fori_loop(0, count // CHUNK, some, 0)

    steps.corner(0)
    for load in loads:
        load.wait()
    input_rows((1 - rank) * count, leaving)
    swapped = steps.remote(leaving, arrived_ref, swap_sem, steps.across)
    swapped.start()
    for step in range(steps.depth + 2):
        if 1 <= step < steps.depth:
            steps.corner(step)
        if 1 <= step <= steps.depth:
            steps.plane(step - 1)
        if step == 1:
            input_rows(rank * count, mine_ref)
        if step >= 2:
            steps.ring(step - 2)
    swapped.wait_recv()
    swapped.wait_send()
    steps.finish()


def reduce_blocks(own, other, head_grads, own_weight, other_weight, back, size, cut):
    slot = own[0].shape[0] // size
    widths = tuple(value.shape[1] for value in own)
    half = (back.shape[0] // 2, back.shape[1])
    blocks = [value.reshape(size, slot, value.shape[1]) for value in (*own, *other)]
    any_spec = pl.BlockSpec(memory_space=pl.ANY)
    vmem_spec = pl.BlockSpec(memory_space=pltpu.VMEM)
    *totals, arrived, mine = pl.pallas_call(
        functools.partial(reduce_kernel, size, cut, widths),
        in_specs=[any_spec] * (len(blocks) + 3) + [vmem_spec],
        out_specs=[vmem_spec] * (len(widths) + 2) + [any_spec, vmem_spec],
        out_shape=[jax.ShapeDtypeStruct((slot, width), F32) for width in (*widths[:-1], *[widths[-1] // 3] * 3)]
        + [jax.ShapeDtypeStruct(half, BF), jax.ShapeDtypeStruct(half, F32)],
        scratch_shapes=[
            pltpu.SemaphoreType.DMA((2,)),
            pltpu.SemaphoreType.DMA((3,)),
            pltpu.VMEM(head_grads.shape, BF),
            pltpu.VMEM((2, own_weight.shape[0], widths[-1]), BF),
            pltpu.VMEM(half, BF),
        ]
        + reducer_scratch(size, slot, cut, widths),
        compiler_params=pltpu.CompilerParams(
            collective_id=1, has_side_effects=True, vmem_limit_bytes=VMEM_LIMIT
        ),
        name="reduce_blocks",
    )(*blocks, head_grads, own_weight, other_weight, back)
    return totals, arrived, mine


PLAN = {
    1: (("corner", 0),),
    2: (("corner", 1), ("corner", 2)),
    3: (("plane", 0), ("corner", 3)),
    4: (("plane", 1),),
    5: (("plane", 2),),
    6: (("plane", 3),),
    7: (("ring", 0),),
    9: (("ring", 1),),
    11: (("ring", 2),),
}


def backward_reduce_kernel(size, cut, widths, flip_ref, bias_ref, *refs):
    own_refs, other_refs = refs[:4], refs[4:8]
    parts = refs[8:12]
    dqkv_ref, outer_ref, inner_ref = refs[12:15]
    work, own_scratch, scratch = refs[15:19], refs[19:24], refs[24:]
    moves = ((outer_ref, 0, 0, widths[0]), (inner_ref, 0, widths[0], widths[1]))
    steps = Reducer(size, cut, widths, parts[:2], parts[2:], moves, scratch)
    at = pl.program_id(0)
    last = pl.num_programs(0) - 1
    pairs = pl.num_programs(0) // 2

    def fill(sources):
        for target, source in zip(work, sources):
            target[...] = source[...]

    @pl.when(at < pairs)
    def _():
        fill(own_refs)

    @pl.when(at >= pairs)
    def _():
        fill(other_refs)

    def hook(head):
        for point, moves in PLAN.items():
            if point % 2 == head:

                @pl.when(at == point // 2)
                def _(moves=moves):
                    for name, age in moves:
                        getattr(steps, name)(age)

    def before():
        @pl.when(at == 0)
        def _():
            steps.start()

        hook(0)

    qkv_ref, grad_ref, out_ref, lse_ref = work
    backward_kernel(
        flip_ref, qkv_ref, bias_ref, grad_ref, out_ref, lse_ref,
        dqkv_ref.at[0], *own_scratch, (before, functools.partial(hook, 1)),
    )

    @pl.when(at == last)
    def _():
        steps.ring(3)
        steps.finish()


def attention_backward_reduce(flips, qkv, bias, grads, outs, lse, own, other, size, cut):
    width = qkv[0].shape[1] // 3
    pairs = width // LANES
    slot = own[0].shape[0] // size
    widths = tuple(value.shape[1] for value in own)
    blocks = [value.reshape(size, slot, value.shape[1]) for value in (*own, *other)]
    any_spec = pl.BlockSpec(memory_space=pl.ANY)

    def half_specs(index):
        return [
            pl.BlockSpec((GROUP_TOK, 3 * LANES), lambda i: (0, index(i))),
            pl.BlockSpec((GROUP_TOK, LANES), lambda i: (0, index(i))),
            pl.BlockSpec((GROUP_TOK, LANES), lambda i: (0, index(i))),
            pl.BlockSpec((1, 8, GROUP_TOK), lambda i: (index(i), 0, 0)),
        ]

    return pl.pallas_call(
        functools.partial(backward_reduce_kernel, size, cut, widths),
        grid=(2 * pairs,),
        in_specs=[
            flip_spec(),
            bias_spec(),
            *half_specs(lambda i: jnp.minimum(i, pairs - 1)),
            *half_specs(lambda i: jnp.maximum(i - pairs, 0)),
            *[any_spec] * 4,
        ],
        out_specs=[
            pl.BlockSpec((1, GROUP_TOK, 3 * LANES), lambda i: (i // pairs, 0, i % pairs)),
            *[pl.BlockSpec((slot, value), lambda i: (0, 0)) for value in widths],
        ],
        out_shape=[
            jax.ShapeDtypeStruct((2, GROUP_TOK, 3 * width), BF),
            *[jax.ShapeDtypeStruct((slot, value), F32) for value in widths],
        ],
        scratch_shapes=[
            pltpu.VMEM((GROUP_TOK, 3 * LANES), BF),
            pltpu.VMEM((GROUP_TOK, LANES), BF),
            pltpu.VMEM((GROUP_TOK, LANES), BF),
            pltpu.VMEM((1, 8, GROUP_TOK), F32),
        ]
        + backward_scratch()
        + reducer_scratch(size, slot, cut, widths),
        compiler_params=pltpu.CompilerParams(
            collective_id=2, has_side_effects=True, vmem_limit_bytes=VMEM_LIMIT
        ),
        name="attention_backward_reduce",
    )(
        jnp.concatenate(flips),
        bias,
        qkv[0], grads[0], outs[0], lse[0],
        qkv[1], grads[1], outs[1], lse[1],
        *blocks,
    )


def swap_pair(value):
    return lax.ppermute(value, "tensor", [(0, 1), (1, 0)])


def swap_bit(value, bit, size):
    return lax.ppermute(value, "dp", [(i, i ^ (1 << bit)) for i in range(size)])


def pick(stacked, index, axis=0):
    return lax.dynamic_index_in_dim(stacked, index, axis, keepdims=False)


def reduce_tree(own, other, order, size, last_type=F32):
    bits = size.bit_length() - 1
    me = lax.axis_index("dp")
    held = [value.reshape((2,) * bits + (value.shape[0] // size,) + value.shape[1:]) for value in (own, other)]
    left = list(range(bits - 1, -1, -1))
    for step, move in enumerate(order):
        kind = last_type if step == len(order) - 1 else own.dtype
        if move == "t":
            arrived = swap_pair(held[1])
            held = [(held[0].astype(F32) + arrived.astype(F32)).astype(kind)]
            continue
        axis = left.index(move)
        left.remove(move)
        mine = lax.rem(lax.div(me, 1 << move), 2)
        arrived = [swap_bit(pick(value, 1 - mine, axis), move, size) for value in held]
        held = [
            (pick(value, mine, axis).astype(F32) + got.astype(F32)).astype(kind)
            for value, got in zip(held, arrived)
        ]
    return held[0]


def tree_order(size, pair_first):
    bits = size.bit_length() - 1
    rest = list(range(bits - 1, 1, -1))
    if pair_first:
        return [0, "t", 1] + rest
    return [0, 1, "t"] + rest


def local(
    inputs,
    cotangent,
    seg_ids,
    block_perm,
    query_weight,
    key_weight,
    value_weight,
    output_weight,
    inner_weight,
    outer_weight,
    first_gain,
    first_shift,
    second_gain,
    second_shift,
    size,
):
    rank = lax.axis_index("tensor")
    at_first = rank == 0

    def both(stacked):
        return pick(stacked, rank), pick(stacked, 1 - rank)

    width = query_weight.shape[1]
    hidden_width = inner_weight.shape[1]
    slot = query_weight.shape[0]
    vectors = jnp.concatenate([first_gain, first_shift, second_gain, second_shift])
    per_vector = first_gain.shape[0]
    order = block_perm.reshape(-1).astype(BF)
    vector_block = jnp.concatenate(
        [jnp.pad(value[None, :], ((0, 0), (0, 128 - value.shape[0]))) for value in (vectors, order)]
        + [jnp.zeros((slot - 2, 128), BF)]
    )
    pieces = [query_weight, key_weight, value_weight, output_weight.T, vector_block, inner_weight, outer_weight.T]
    plan = [
        [(pair * LANES, (3 * pair + index) * LANES, LANES) for pair in range(width // LANES)] for index in range(3)
    ]
    reached = 3 * width
    for piece in pieces[3:]:
        plan.append([(0, reached, piece.shape[1])])
        reached += piece.shape[1]
    own, other, arrived_rows = gather_weights(pieces, plan, inputs, size)
    flat = [value.reshape(-1, value.shape[-1]) for value in (own, other)]
    edges = [0, 3 * width, 4 * width, 4 * width + 128, 4 * width + 128 + hidden_width, reached]
    w_qkv, w_output, vector_rows, w_inner, w_outer = [
        [value[:, low:high] for value in flat] for low, high in zip(edges[:-1], edges[1:])
    ]
    perms = [value[1, : order.shape[0]].astype(jnp.int32).reshape(block_perm.shape) for value in vector_rows]
    vector_rows = [value.reshape(size, slot, 128)[:, 0, : 4 * per_vector] for value in vector_rows]
    all_vectors = jnp.stack(
        [jnp.where(at_first, *vector_rows), jnp.where(at_first, *vector_rows[::-1])], axis=1
    )
    all_vectors = all_vectors.reshape(size, 2, 4, per_vector).transpose(2, 0, 1, 3).reshape(4, -1)
    gain_one, shift_one, gain_two, shift_two = [all_vectors[i].astype(F32) for i in range(4)]

    def collect(mine_and_other, arrived):
        mine = pick(mine_and_other, rank)
        return jnp.concatenate(
            [jnp.where(at_first, mine, arrived), jnp.where(at_first, arrived, mine)], axis=0
        )

    def lay(mine, arrived):
        both_rows = jnp.broadcast_to(arrived.astype(mine.dtype)[None], (2,) + mine.shape)
        return lax.dynamic_update_slice(both_rows, mine[None], (rank, 0, 0))

    rows = collect(inputs, arrived_rows)
    segments = pick(seg_ids, rank)[0]
    bias = jnp.where(segments[:, None] == segments[None, :], 0.0, MASKED).astype(F32)

    qkv = [matmul(rows, weight).astype(BF) for weight in w_qkv]
    qkv[0], late = lax.optimization_barrier((qkv[0], pick(cotangent, 1 - rank)))
    late = swap_pair(late)
    attended, lse = zip(*[attention_forward(p, value, bias) for p, value in zip(perms, qkv)])
    attention_sum = contract_cols(attended[0], w_output[0]) + contract_cols(attended[1], w_output[1])
    attention_sum, late = lax.optimization_barrier((attention_sum, late))
    upstream = collect(cotangent, late).astype(F32)
    hidden, unit_one, inverse_one = normalize(rows.astype(F32) + attention_sum, gain_one, shift_one)
    hidden_low = hidden.astype(BF)
    activated, slope = zip(*[gelu_pair(matmul(hidden_low, weight)) for weight in w_inner])
    activated = [value.astype(BF) for value in activated]
    slope = list(lax.optimization_barrier([value.astype(BF) for value in slope]))
    branch = contract_cols(activated[0], w_outer[0]) + contract_cols(activated[1], w_outer[1])
    layer_out, unit_two, inverse_two = normalize(hidden + branch, gain_two, shift_two)
    layer_low = layer_out.astype(BF)
    layer_leaving = pick(layer_low.reshape(4, -1, layer_low.shape[1]).reshape(2, 2, -1, layer_low.shape[1]), 1 - rank)
    layer_first = swap_pair(layer_leaving[0])

    second_back = normalize_back(upstream, unit_two, inverse_two, gain_two)
    branch_grad = second_back.astype(BF)
    outer_terms = [contract_rows(branch_grad, value).astype(BF) for value in activated]
    pre_grad = [
        (matmul(branch_grad, weight) * part.astype(F32)).astype(BF) for weight, part in zip(w_outer, slope)
    ]
    layer_first, pre_grad[1] = lax.optimization_barrier((layer_first, pre_grad[1]))
    layer_second, layer_first = lax.optimization_barrier((layer_leaving[1], layer_first))
    layer_second = swap_pair(layer_second)
    inner_terms = [contract_rows(hidden_low, value).astype(BF) for value in pre_grad]
    hidden_back = second_back + contract_cols(pre_grad[0], w_inner[0]) + contract_cols(pre_grad[1], w_inner[1])
    first_back = normalize_back(hidden_back, unit_one, inverse_one, gain_one)
    norm_terms = jnp.stack(
        [
            jnp.sum(hidden_back * unit_one, axis=0),
            jnp.sum(hidden_back, axis=0),
            jnp.sum(upstream * unit_two, axis=0),
            jnp.sum(upstream, axis=0),
        ]
    )
    by_shard = norm_terms.reshape(4, size, 2, per_vector).transpose(2, 1, 0, 3).reshape(2, size, 4, per_vector)
    vector_terms = [
        jnp.pad(value.reshape(size, 1, 4 * per_vector), ((0, 0), (0, slot - 1), (0, 128 - 4 * per_vector)))
        .reshape(size * slot, 128)
        .astype(BF)
        for value in both(by_shard)
    ]

    attention_grad = first_back.astype(BF)
    output_terms = [contract_rows(attention_grad, value).astype(BF) for value in attended]
    attended_grad = [matmul(attention_grad, weight).astype(BF) for weight in w_output]
    layer_second, attended_grad[0] = lax.optimization_barrier((layer_second, attended_grad[0]))
    layer_arrived = jnp.concatenate([layer_first, layer_second])
    layer_rows = lay(pick(layer_low.reshape(2, -1, layer_low.shape[1]), rank), layer_arrived)
    flips = [
        jnp.broadcast_to(
            jnp.pad(value[:, 0].astype(F32).reshape(-1, 2), ((0, 0), (0, 6)))[:, :, None],
            (value.shape[0] // 2, 8, HALF),
        )
        for value in perms
    ]
    fast = size == 16 and slot % 16 == 0
    if fast:
        head_grads, grad_outer, grad_inner = attention_backward_reduce(
            flips, qkv, bias, attended_grad, attended, lse, *zip(outer_terms, inner_terms), size, BACK_CUT
        )
    else:
        operands = zip(flips, qkv, [bias] * 2, attended_grad, attended, lse)
        head_grads = [attention_backward(*values) for values in operands]
    head_terms = [contract_rows(rows, value).astype(BF) for value in head_grads]
    terms = list(zip(output_terms, vector_terms, head_terms))
    if fast:
        (grad_output, norm_rows, grad_query, grad_key, grad_value), arrived, mine = reduce_blocks(
            *terms, head_grads, *flat, first_back, size, REDUCE_CUT
        )
    else:
        terms = [(outer, inner, *rest) for outer, inner, rest in zip(outer_terms, inner_terms, terms)]
        packed = [jnp.concatenate(value, axis=1) for value in terms]
        total = reduce_tree(*packed, tree_order(size, True), size).reshape(slot, -1)
        input_grad = first_back + contract_cols(head_grads[0], w_qkv[0]) + contract_cols(head_grads[1], w_qkv[1])
        halves = input_grad.reshape(2, GROUP_TOK // 2, -1)
        mine, arrived = pick(halves, rank), swap_pair(pick(halves, 1 - rank).astype(BF))
        edges = [0]
        for value in terms[0]:
            edges.append(edges[-1] + value.shape[1])
        grad_outer, grad_inner, grad_output, norm_rows, grad_heads = [
            total[:, low:high] for low, high in zip(edges[:-1], edges[1:])
        ]
        grad_heads = grad_heads.reshape(slot, -1, 3, LANES)
        grad_query, grad_key, grad_value = [grad_heads[:, :, i].reshape(slot, width) for i in range(3)]
    input_rows = lay(mine, arrived)
    norm_shards = norm_rows[0, : 4 * per_vector].reshape(4, per_vector)
    return (
        layer_rows,
        input_rows,
        grad_query,
        grad_key,
        grad_value,
        grad_output.T,
        grad_inner,
        grad_outer.T,
        norm_shards[0],
        norm_shards[1],
        norm_shards[2],
        norm_shards[3],
    )


def solution(mesh):
    rows = P(None, ("dp", "tensor"), None)
    columns = P("dp", "tensor")
    flipped = P("tensor", "dp")
    vector = P(("dp", "tensor"))
    return jax.shard_map(
        functools.partial(local, size=mesh.shape["dp"]),
        mesh=mesh,
        in_specs=(
            rows, rows, P(None, "dp", None), P("tensor", None),
            columns, columns, columns, flipped, columns, flipped,
            vector, vector, vector, vector,
        ),
        out_specs=(
            rows, rows, columns, columns, columns, flipped, columns, flipped,
            vector, vector, vector, vector,
        ),
        check_vma=False,
    )
```
